512 devices in a mesh: wide: 64 (over y, z_lo, core), narrow: 8 (over x, z_hi).
Axes of the slice: x: 4, y: 8, z: 8 (z_hi: 2, z_lo: 4; z = z_hi * 4 + z_lo), core: 2. Of those that a mesh axis runs over, the one named last changes fastest.
Arguments:
- loads: float32 [2048, 24, 128], P(('wide', 'narrow')), may hold values from -6 to 6
- diagonal: float32 [2048, 128], P(('wide', 'narrow')), may hold values from 2 to 7
- stiffness: float32 [2048, 4, 128, 128], P(('wide', 'narrow')), may hold values from 0 to 0.001953125
- neighbors: int32 [2048, 4], P(('wide', 'narrow')), may hold values from 0 to 7
- slot_mask: int32 [2048, 4], P(('wide', 'narrow')), may hold values 0 or 1
- send_list: int32 [2048], P(('wide', 'narrow')), may hold values from 0 to 3
- aggregate: int32 [2048, 128], P(('wide', 'narrow')), may hold values from 0 to 127
- coarse_inverse: float32 [8192, 8192], P(('wide', 'narrow')), may hold values from -0.0078125 to 0.0078125
Outputs:
- correction: float32 [2048, 24, 128], P(('wide', 'narrow'))
- residual: float32 [2048, 24, 128], P(('wide', 'narrow'))
The draws below stay inside these ranges and needn't reach their ends.
Inputs may be any that keep to these rules, and one draw needn't show every extreme that they name: `neighbors`: indices into the extended list of the block's group. `send_list`: block indices within the sending group. aggregate indices among the 128 aggregates of the particle's wide coordinate.
All inputs are finite; a program needn't handle non-finite values. No bound on the sum of `slot_mask` on one device may be relied on, other than what follows from the above.
Results may differ from the reference program's by a relative error of at most 0.00025.
Values sent between devices are 32-bit elements; how exact they have to be, the bound alone decides.
A program may use at most 64 MiB of HBM per device.

```python
import jax
import jax.numpy as jnp
from jax import lax

BS = 128
NB = 4
NS = 4
SWEEPS = 2
AGG_DEV = 16
GHOST = 2
VEC = 24
BLOCKS = 2048
SENDS = 2048
AGG_W = 128
NC = 8192
N_WIDE = 64
N_NARROW = 8


def draw_diagonal(key, part):
    count = BLOCKS * BS
    place = jnp.arange(count, dtype=jnp.float32).reshape(BLOCKS, BS) / max(count - 1, 1)
    level = 3.0 - 2.0 * place
    spread = jax.random.uniform(key, (BLOCKS, BS), jnp.float32)
    return (1.0 + level * (1.0 + spread)).astype(jnp.float32)


def plant(array, stream_key, smallest, top_value):
    spot = [jax.random.randint(jax.random.fold_in(stream_key, axis), (), 0, length) for axis, length in enumerate(array.shape)]
    widest = array.shape.index(max(array.shape))
    beside = spot[:widest] + [(spot[widest] + 1) % array.shape[widest]] + spot[widest + 1:]
    return array.at[tuple(spot)].set(smallest).at[tuple(beside)].set(top_value)


def shard_levels(own_key, dims, shards, least, high):
    gain = 1.0
    for axis_at, shards_of in shards:
        draws = jax.random.uniform(jax.random.fold_in(jax.random.fold_in(own_key, 6), axis_at), (shards_of,), jnp.float32, least / len(shards), high / len(shards))
        gain = gain * jnp.repeat(jnp.exp(draws), dims[axis_at] // shards_of).reshape((-1,) + (1,) * (len(dims) - 1 - axis_at))
    return gain


def gaussian(stream_key, dims, deviation, limit, cuts=(), kind=jnp.bfloat16):
    array = deviation * jax.random.normal(stream_key, dims, jnp.float32)
    if cuts:
        array = array * shard_levels(stream_key, dims, cuts, -0.22, 0.18)
    return jnp.clip(array, -limit, limit).astype(kind)


def setup_inputs(seed: int = 0) -> dict:
    keys = jax.random.split(jax.random.key(seed), 9)
    return {
        "loads": gaussian(keys[0], (BLOCKS, VEC, BS), 1.0, 6.0, ((0, 512),), jnp.float32),
        "diagonal": draw_diagonal(jax.random.fold_in(keys[8], 71), 0),
        "stiffness": jnp.clip(0.001953125 * jax.random.uniform(keys[2], (BLOCKS, NS, BS, BS), jnp.float32) ** shard_levels(keys[2], (BLOCKS, NS, BS, BS), ((0, 512),), -0.2, 0.2), 0.0, 0.001953125),
        "neighbors": plant(jax.random.randint(keys[3], (BLOCKS, NS), 0, NB + 2 * GHOST), jax.random.fold_in(keys[3], 1), 0, (NB + 2 * GHOST) - 1).astype(jnp.int32),
        "slot_mask": plant((jax.random.randint(keys[4], (BLOCKS, NS), 0, 4) < 3).astype(jnp.int32), jax.random.fold_in(keys[4], 1), 0, 1),
        "send_list": plant(jax.random.randint(keys[5], (SENDS,), 0, NB), jax.random.fold_in(keys[5], 1), 0, NB - 1).astype(jnp.int32),
        "aggregate": plant(jax.random.randint(keys[6], (BLOCKS, BS), 0, AGG_DEV * N_NARROW), jax.random.fold_in(keys[6], 1), 0, (AGG_DEV * N_NARROW) - 1).astype(jnp.int32),
        "coarse_inverse": gaussian(keys[7], (NC, NC), (NC * 64) ** -0.5, 0.0078125, ((0, 512),), jnp.float32),
    }


highest = lax.Precision.HIGHEST


def extended_lists(send_list):
    groups = N_WIDE * N_NARROW
    sending = send_list.reshape(groups, 2 * GHOST)
    group_ids = jnp.arange(groups, dtype=jnp.int32)
    wide_ids = group_ids // N_NARROW
    own_blocks = group_ids[:, None] * NB + jnp.arange(NB, dtype=jnp.int32)[None, :]
    left_group = jnp.clip(group_ids - N_NARROW, 0, groups - 1)
    right_group = jnp.clip(group_ids + N_NARROW, 0, groups - 1)
    left_blocks = left_group[:, None] * NB + sending[left_group, GHOST:]
    right_blocks = right_group[:, None] * NB + sending[right_group, :GHOST]
    index_table = jnp.concatenate([own_blocks, left_blocks, right_blocks], axis=1).astype(jnp.int32)
    left_valid = jnp.broadcast_to((wide_ids > 0)[:, None], (groups, GHOST))
    right_valid = jnp.broadcast_to((wide_ids < N_WIDE - 1)[:, None], (groups, GHOST))
    own_valid = jnp.ones((groups, NB), jnp.bool_)
    valid_table = jnp.concatenate([own_valid, left_valid, right_valid], axis=1).astype(jnp.float32)
    return index_table, valid_table


def reference(loads, diagonal, stiffness, neighbors, slot_mask, send_list, aggregate, coarse_inverse):
    groups = N_WIDE * N_NARROW
    index_table, valid_table = extended_lists(send_list)
    grouped = neighbors.reshape(groups, NB * NS).astype(jnp.int32)
    global_nbr = jnp.take_along_axis(index_table, grouped, axis=1).reshape(BLOCKS, NS)
    live_slots = slot_mask.astype(jnp.float32)
    weights_live = jnp.take_along_axis(valid_table, grouped, axis=1).reshape(BLOCKS, NS) * live_slots
    diag_rows = diagonal[:, None, :]

    def operate(vector):
        gathered = vector[global_nbr] * weights_live[:, :, None, None]
        coupled = jnp.einsum("bscj,bsij->bci", gathered, stiffness, precision=highest)
        return diag_rows * vector - coupled

    row_abs = lax.map(lambda block_group: jnp.sum(jnp.abs(block_group), axis=3),
                      stiffness.reshape(groups, NB, NS, BS, BS)).reshape(BLOCKS, NS, BS)
    row_ratio = jnp.sum(row_abs * live_slots[:, :, None], axis=1) / diagonal
    upper_bound = 1.0 + jnp.max(row_ratio)
    centre = 0.625 * upper_bound
    half_span = 0.375 * upper_bound
    spread_ratio = 5.0 / 3.0
    weight_prev = 0.6
    direction = (loads / diag_rows) / centre
    solution = direction
    remainder = loads
    for sweep_index in range(SWEEPS):
        remainder = remainder - operate(direction)
        weight_now = 1.0 / (2.0 * spread_ratio - weight_prev)
        direction = (weight_now * weight_prev) * direction + ((2.0 * weight_now / half_span) * remainder) / diag_rows
        solution = solution + direction
        weight_prev = weight_now
    residual = remainder - operate(direction)
    wide_of_block = jnp.arange(BLOCKS, dtype=jnp.int32) // (NB * N_NARROW)
    global_agg = (wide_of_block[:, None] * AGG_W + aggregate).astype(jnp.int32)
    flat_res = jnp.transpose(residual, (0, 2, 1)).reshape(BLOCKS * BS, VEC)
    coarse_rhs = jax.ops.segment_sum(flat_res, global_agg.reshape(-1), num_segments=NC)
    coarse_sol = jnp.dot(coarse_inverse, coarse_rhs, precision=highest, preferred_element_type=jnp.float32)
    spread_back = jnp.transpose(coarse_sol[global_agg], (0, 2, 1))
    return solution + spread_back, residual
```

```python
import jax
import jax.numpy as jnp
from jax import lax
from jax.experimental import pallas as pl
from jax.experimental.pallas import tpu as pltpu
from jax.sharding import PartitionSpec as P

F32 = jnp.float32
BF16 = jnp.bfloat16
MESH = pl.DeviceIdType.MESH
NB, NS, VEC, BS = 4, 4, 24, 128
NX, NY, NZL, NZH = 4, 8, 4, 2
NZ = NZL * NZH
NQ = 2 * NX
N_WIDE = NY * NZL * 2
SWEEPS = 2
ROWS = 16
NT = (((1,), (1,)), ((), ()))
NN = (((1,), (0,)), ((), ()))


def split(value):
    high = value.astype(BF16).astype(F32)
    return jnp.concatenate([high, value - high], axis=0).astype(BF16)


def dot(a, b, dims):
    return lax.dot_general(a, b, dims, preferred_element_type=F32)


def folded(full):
    half = full.shape[0] // 2
    cols = full.shape[1] // 2
    return full[:half, :cols] + (full[:half, cols:] + full[half:, :cols])


def kernel(nbr, msk, snd, loads_h, diag_h, stiff_h, agg_h, inv_h, corr_h, res_h,
           loads_v, diag_v, stiff_v, agg_v, inv_v, own, ksum, sbuf, ghost, exts, w2,
           mx, inv_s, inv_r, wc, oh, ohs, p_s, a_r, b_r, c_r, d_r, e_r, res_v, corr_v,
           lsem, halo_ss, halo_rs, mx_ss, mx_rs, inv_ss, inv_rs, a_ss, a_rs, b_ss, b_rs,
           c_ss, c_rs, d_ss, d_rs, e_ss, e_rs):
    w = lax.axis_index("wide")
    n = lax.axis_index("narrow")
    core = w % 2
    zl = (w // 2) % NZL
    y = w // (2 * NZL)
    x = n // NZH
    zh = n % NZH
    z = zh * NZL + zl
    q = 2 * x + core

    def at(y_, zl_, core_, x_, zh_):
        return ((y_ * NZL + zl_) * 2 + core_, x_ * NZH + zh_)

    def xk_peer(d):
        other = (q + d) % NQ
        return at(y, zl, other % 2, other // 2, zh)

    def z_peer(d):
        other = (z + d) % NZ
        return at(y, other % NZL, core, x, other // NZL)

    def y_peer(d):
        return at((y + d) % NY, zl, core, x, zh)

    def rcopy(src, dst, ss, rs, dev):
        return pltpu.make_async_remote_copy(src_ref=src, dst_ref=dst, send_sem=ss, recv_sem=rs,
                                            device_id=dev, device_id_type=MESH)

    barrier = pltpu.get_barrier_semaphore()

    def greet(dev):
        pl.semaphore_signal(barrier, inc=1, device_id=dev, device_id_type=MESH)

    left_far = jnp.logical_and(core == 0, w > 0)
    right_far = jnp.logical_and(core == 1, w < N_WIDE - 1)
    pl.when(left_far)(lambda: greet((w - 1, n)))
    pl.when(right_far)(lambda: greet((w + 1, n)))
    for d in range(1, 8):
        greet(xk_peer(d))
        greet(z_peer(d))
        greet(y_peer(d))

    cp_loads = pltpu.make_async_copy(loads_h, loads_v, lsem.at[0])
    cp_diag = pltpu.make_async_copy(diag_h, diag_v, lsem.at[1])
    cp_stiff = [pltpu.make_async_copy(stiff_h.at[b], stiff_v.at[b], lsem.at[2 + b]) for b in range(NB)]
    cp_inv = pltpu.make_async_copy(inv_h, inv_v, lsem.at[6])
    cp_agg = pltpu.make_async_copy(agg_h, agg_v, lsem.at[7])
    for cp in [cp_loads, cp_diag] + cp_stiff + [cp_inv, cp_agg]:
        cp.start()

    @pl.when(w == 0)
    def _():
        ghost[:, 0:2] = jnp.zeros((3, 2, VEC, BS), F32)

    @pl.when(w == N_WIDE - 1)
    def _():
        ghost[:, 2:4] = jnp.zeros((3, 2, VEC, BS), F32)

    cp_loads.wait()
    cp_diag.wait()
    rdiag = [1.0 / diag_v[b:b + 1, :] for b in range(NB)]
    for b in range(NB):
        own[0, b] = loads_v[b] * rdiag[b]

    def to_left(k):
        return rcopy(sbuf.at[k, pl.ds(0, 2)], ghost.at[k, pl.ds(2, 2)], halo_ss.at[k, 0], halo_rs.at[k, 0], (w - 1, n))

    def to_right(k):
        return rcopy(sbuf.at[k, pl.ds(2, 2)], ghost.at[k, pl.ds(0, 2)], halo_ss.at[k, 1], halo_rs.at[k, 1], (w + 1, n))

    def send_halo(k):
        for j in range(4):
            sbuf[k, j] = own[k, snd[j]]
        pl.when(w > 0)(lambda: to_left(k).start())
        pl.when(w < N_WIDE - 1)(lambda: to_right(k).start())

    def wait_halo(k):
        pl.when(w < N_WIDE - 1)(lambda: to_left(k).wait_recv())
        pl.when(w > 0)(lambda: to_right(k).wait_recv())

    @pl.when(jnp.logical_or(left_far, right_far))
    def _():
        pl.semaphore_wait(barrier, 22)

    @pl.when(jnp.logical_not(jnp.logical_or(left_far, right_far)))
    def _():
        pl.semaphore_wait(barrier, 21)

    send_halo(0)

    ones = jnp.ones((8, BS), F32)
    peak = None
    for b in range(NB):
        cp_stiff[b].wait()
        total = None
        for s in range(NS):
            block = stiff_v[b, s] * msk[b, s].astype(F32)
            size = jnp.abs(block)
            total = size if total is None else total + size
            high = block.astype(BF16)
            w2[b, 0:BS, s * BS:(s + 1) * BS] = high
            w2[b, BS:2 * BS, s * BS:(s + 1) * BS] = (block - high.astype(F32)).astype(BF16)
        sums = lax.dot_general(ones, total, NT, precision=lax.Precision.HIGHEST, preferred_element_type=F32)
        ratio = sums / diag_v[b:b + 1, :]
        peak = ratio if peak is None else jnp.maximum(peak, ratio)
    mx[0, 0] = jnp.broadcast_to(jnp.max(peak, axis=1, keepdims=True), (8, BS))

    def peak_copy(stage, d):
        dev = (xk_peer, z_peer, y_peer)[stage](d)
        return rcopy(mx.at[stage, 0], mx.at[stage, d], mx_ss.at[stage, d], mx_rs.at[stage, d], dev)

    def send_peak(stage):
        for d in range(1, 8):
            peak_copy(stage, d).start()

    def take_peak(stage):
        for d in range(1, 8):
            peak_copy(stage, d).wait_recv()
        top = mx[stage, 0]
        for d in range(1, 8):
            top = jnp.maximum(top, mx[stage, d])
        return top

    send_peak(0)

    def split_own(k):
        for b in range(NB):
            exts[b] = split(own[k, b])

    split_own(0)

    cp_inv.wait()
    for j in range(NQ):
        for i in range(NY):
            col = (NQ * i + j) * BS
            inv_s[j, i] = inv_v[:, col:col + BS]

    def inv_copy(d):
        other = (q + d) % NQ
        return rcopy(inv_s.at[other], inv_r.at[q], inv_ss.at[d], inv_rs.at[d], xk_peer(d))

    for d in range(1, NQ):
        inv_copy(d).start()
    inv_r[q] = inv_s[q]

    def couple(k):
        wait_halo(k)
        for j in range(4):
            exts[NB + j] = split(ghost[k, j])
        for b in range(NB):
            fields = jnp.concatenate([exts[nbr[b, s]] for s in range(NS)], axis=1)
            coupled = folded(dot(fields, w2[b], NT))
            ksum[k, b] = coupled
            if k < SWEEPS:
                own[k + 1, b] = coupled * rdiag[b]
        if k < SWEEPS:
            send_halo(k + 1)

    couple(0)
    mx[1, 0] = take_peak(0)
    send_peak(1)
    split_own(1)

    cp_agg.wait()
    row = lax.broadcasted_iota(jnp.int32, (BS, BS), 0)
    for b in range(NB):
        which = agg_v[b:b + 1, :]
        cols = slice(b * BS, (b + 1) * BS)
        oh[:, cols] = jnp.where(row == which, 1.0, 0.0).astype(BF16)
        for side in range(NZH):
            target = jnp.where((row // 16) % 2 == core, 32 * (row // 32) + 16 * side + row % 16, -1)
            ohs[side, :, cols] = jnp.where(target == which, 1.0, 0.0).astype(BF16)

    couple(1)
    mx[2, 0] = take_peak(1)
    send_peak(2)
    split_own(2)

    for d in range(1, NQ):
        inv_copy(d).wait_recv()
    for j in range(NQ):
        for i in range(NY):
            block = inv_r[j, i]
            high = block.astype(BF16)
            cols = slice(i * BS, (i + 1) * BS)
            wc[j * ROWS:(j + 1) * ROWS, cols] = high
            wc[BS + j * ROWS:BS + (j + 1) * ROWS, cols] = (block - high.astype(F32)).astype(BF16)

    couple(2)
    upper = 1.0 + take_peak(2)[0:1, :]

    centre = 0.625 * upper
    half_span = 0.375 * upper
    spread_ratio = 5.0 / 3.0
    weight_prev = 0.6
    zero = jnp.zeros_like(upper)
    delta = [1.0 / centre, zero, zero]
    sigma = list(delta)
    rho = [zero + 1.0, zero, zero, zero]

    def apply(rho, delta):
        rho = list(rho)
        for j in range(3):
            rho[j] = rho[j] - delta[j]
            rho[j + 1] = rho[j + 1] + delta[j]
        return rho

    for _ in range(SWEEPS):
        rho = apply(rho, delta)
        weight = 1.0 / (2.0 * spread_ratio - weight_prev)
        gain = 2.0 * weight / half_span
        delta = [weight * weight_prev * delta[j] + gain * rho[j] for j in range(3)]
        sigma = [sigma[j] + delta[j] for j in range(3)]
        weight_prev = weight
    rho = apply(rho, delta)

    parts = []
    for b in range(NB):
        residual = rho[0] * loads_v[b] + rho[1] * ksum[0, b] + rho[2] * ksum[1, b] + rho[3] * ksum[2, b]
        res_v[b] = residual
        parts.append(split(residual))
    pair = dot(jnp.concatenate(parts, axis=1), oh[...], NT)
    part = pair[:VEC] + pair[VEC:]

    slot = (x - zl + NX) % NX
    a_copy = rcopy(p_s, a_r.at[slot], a_ss, a_rs.at[slot], at(y, zl, core, zl, zh))
    owner = x == zl

    def b_copy(d):
        return rcopy(b_r.at[zh], b_r.at[zh], b_ss.at[d], b_rs.at[zh], z_peer(d))

    def b_arrival(side):
        return rcopy(b_r.at[side], b_r.at[side], b_ss.at[0], b_rs.at[side], z_peer(1))

    p_s[...] = part

    @pl.when(jnp.logical_not(owner))
    def _():
        a_copy.start()

    @pl.when(owner)
    def _():
        total = p_s[...]
        for d in range(1, NX):
            rcopy(p_s, a_r.at[d], a_ss, a_rs.at[d], at(y, zl, core, zl, zh)).wait_recv()
            total = total + a_r[d]
        b_r[zh] = total
        for d in range(1, NZ):
            b_copy(d).start()

    cp_res = pltpu.make_async_copy(res_v, res_h, lsem.at[8])
    cp_res.start()

    @pl.when(owner)
    def _():
        b_arrival(1 - zh).wait_recv()

    @pl.when(jnp.logical_not(owner))
    def _():
        for side in range(NZH):
            b_arrival(side).wait_recv()

    c_r[y] = b_r[0] + b_r[1]

    def c_copy(d):
        return rcopy(c_r.at[y], c_r.at[y], c_ss.at[d], c_rs.at[d], y_peer(d))

    def c_arrival(d):
        came = (y - d + NY) % NY
        return rcopy(c_r.at[came], c_r.at[came], c_ss.at[d], c_rs.at[d], y_peer(d))

    for d in range(1, NY):
        c_copy(d).start()
    for d in range(1, NY):
        c_arrival(d).wait_recv()
    fields = jnp.concatenate([split(c_r[i]) for i in range(NY)], axis=1)
    d_r[0] = folded(dot(fields, wc[...], NT))

    def d_copy(d):
        return rcopy(d_r.at[0], d_r.at[d], d_ss.at[d], d_rs.at[d], xk_peer(d))

    for d in range(1, NQ):
        d_copy(d).start()
    for d in range(1, NQ):
        d_copy(d).wait_recv()
    total = d_r[0]
    for d in range(1, NQ):
        total = total + d_r[d]
    e_r[0] = total
    e_copy = rcopy(e_r.at[0], e_r.at[1], e_ss, e_rs, at(y, zl, core, x, 1 - zh))
    e_copy.start()

    def spread(values, side):
        pair = dot(split(values), ohs[side], NN)
        return pair[:VEC] + pair[VEC:]

    near = spread(total, zh)
    for b in range(NB):
        corr_v[b] = (sigma[0] * own[0, b] + sigma[1] * own[1, b] + sigma[2] * own[2, b]
                     + near[:, b * BS:(b + 1) * BS])
    e_copy.wait_recv()
    far = spread(e_r[1], 1 - zh)
    for b in range(NB):
        corr_v[b] = corr_v[b] + far[:, b * BS:(b + 1) * BS]
    cp_corr = pltpu.make_async_copy(corr_v, corr_h, lsem.at[9])
    cp_corr.start()

    for k in range(SWEEPS + 1):
        pl.when(w > 0)(lambda k=k: to_left(k).wait_send())
        pl.when(w < N_WIDE - 1)(lambda k=k: to_right(k).wait_send())
    for d in range(1, 8):
        for stage in range(3):
            peak_copy(stage, d).wait_send()
        inv_copy(d).wait_send()
        c_copy(d).wait_send()
        d_copy(d).wait_send()

    @pl.when(owner)
    def _():
        for d in range(1, NZ):
            b_copy(d).wait_send()

    @pl.when(jnp.logical_not(owner))
    def _():
        a_copy.wait_send()

    e_copy.wait_send()
    cp_res.wait()
    cp_corr.wait()


def shards(loads, diagonal, stiffness, neighbors, slot_mask, send_list, aggregate, coarse_inverse):
    smem = pl.BlockSpec(memory_space=pltpu.SMEM)
    hbm = pl.BlockSpec(memory_space=pl.ANY)
    field = (NB, VEC, BS)
    dma = pltpu.SemaphoreType.DMA
    return pl.pallas_call(
        kernel,
        out_shape=(jax.ShapeDtypeStruct(field, F32), jax.ShapeDtypeStruct(field, F32)),
        in_specs=[smem, smem, smem, hbm, hbm, hbm, hbm, hbm],
        out_specs=(hbm, hbm),
        scratch_shapes=[
            pltpu.VMEM(field, F32),
            pltpu.VMEM((NB, BS), F32),
            pltpu.VMEM((NB, NS, BS, BS), F32),
            pltpu.VMEM((NB, BS), jnp.int32),
            pltpu.VMEM((ROWS, NQ * NY * BS), F32),
            pltpu.VMEM((3,) + field, F32),
            pltpu.VMEM((3,) + field, F32),
            pltpu.VMEM((3,) + field, F32),
            pltpu.VMEM((3,) + field, F32),
            pltpu.VMEM((2 * NB, 2 * VEC, BS), BF16),
            pltpu.VMEM((NB, 2 * BS, NS * BS), BF16),
            pltpu.VMEM((3, 8, 8, BS), F32),
            pltpu.VMEM((NQ, NY, ROWS, BS), F32),
            pltpu.VMEM((NQ, NY, ROWS, BS), F32),
            pltpu.VMEM((2 * BS, NY * BS), BF16),
            pltpu.VMEM((BS, NB * BS), BF16),
            pltpu.VMEM((NZH, BS, NB * BS), BF16),
            pltpu.VMEM((VEC, BS), F32),
            pltpu.VMEM((NX, VEC, BS), F32),
            pltpu.VMEM((NZH, VEC, BS), F32),
            pltpu.VMEM((NY, VEC, BS), F32),
            pltpu.VMEM((NQ, VEC, BS), F32),
            pltpu.VMEM((2, VEC, BS), F32),
            pltpu.VMEM(field, F32),
            pltpu.VMEM(field, F32),
            dma((10,)),
            dma((3, 2)), dma((3, 2)),
            dma((3, 8)), dma((3, 8)),
            dma((8,)), dma((8,)),
            dma(()), dma((NX,)),
            dma((8,)), dma((NZH,)),
            dma((8,)), dma((8,)),
            dma((8,)), dma((8,)),
            dma(()), dma(()),
        ],
        compiler_params=pltpu.CompilerParams(collective_id=0, has_side_effects=True, vmem_limit_bytes=24 * 1024 * 1024),
    )(neighbors, slot_mask, send_list, loads, diagonal, stiffness, aggregate, coarse_inverse)


def solution(mesh):
    both = ("wide", "narrow")
    return jax.shard_map(
        shards,
        mesh=mesh,
        in_specs=(
            P(both, None, None),
            P(both, None),
            P(both, None, None, None),
            P(both, None),
            P(both, None),
            P(both),
            P(both, None),
            P(both, None),
        ),
        out_specs=(P(both, None, None), P(both, None, None)),
        check_vma=False,
    )
```

```python
import jax
import jax.numpy as jnp
from jax import lax
from jax.experimental import pallas as pl
from jax.experimental.pallas import tpu as pltpu
from jax.sharding import PartitionSpec as P

F32 = jnp.float32
BF16 = jnp.bfloat16
MESH = pl.DeviceIdType.MESH
NB, NS, VEC, BS = 4, 4, 24, 128
NX, NY, NZL, NZH = 4, 8, 4, 2
NZ = NZL * NZH
NG = 2 * NX
N_WIDE = NY * NZL * 2
SWEEPS = 2
ROWS = 16
NT = (((1,), (1,)), ((), ()))
NN = (((1,), (0,)), ((), ()))


def split(value):
    high = value.astype(BF16).astype(F32)
    return jnp.concatenate([high, value - high], axis=0).astype(BF16)


def dot(a, b, dims):
    return lax.dot_general(a, b, dims, preferred_element_type=F32)


def folded(full):
    half = full.shape[0] // 2
    cols = full.shape[1] // 2
    return full[:half, :cols] + (full[:half, cols:] + full[half:, :cols])


def roll(value, lanes):
    return value if lanes % BS == 0 else pltpu.roll(value, lanes % BS, 1)


def regroup(tiles, count, width):
    lane = lax.broadcasted_iota(jnp.int32, tiles[0].shape, 1) // width
    out = []
    for i in range(count):
        acc = None
        for j, tile in enumerate(tiles):
            moved = roll(tile, width * (j - i))
            acc = moved if acc is None else jnp.where(lane == j, moved, acc)
        out.append(acc)
    return out


def hops(step, size):
    return min(step, size - step)


def kernel(nbr_h, msk_h, snd_h, loads_h, diag_h, stiff_h, agg_h, inv_h, corr_v, res_v,
           nbr, msk, snd, loads_v, diag_v, stiff_v, agg_v, inv_v, own, ksum, sbuf, ghost, exts, w2,
           mx, inv_s, inv_r, wc, oh, ohs, i_s, i_r, c_r, d_s, d_r,
           lsem, halo_ss, halo_rs, mx_ss, mx_rs, inv_ss, inv_rs, i_ss, i_rs, c_ss, c_rs, d_ss, d_rs):
    w = lax.axis_index("wide")
    n = lax.axis_index("narrow")
    core = w % 2
    zl = (w // 2) % NZL
    y = w // (2 * NZL)
    x = n // NZH
    zh = n % NZH
    z = zh * NZL + zl
    g = NX * core + x

    cp_loads = pltpu.make_async_copy(loads_h, loads_v, lsem.at[0])
    cp_diag = pltpu.make_async_copy(diag_h, diag_v, lsem.at[1])
    cp_stiff = [pltpu.make_async_copy(stiff_h.at[b], stiff_v.at[b], lsem.at[2 + b]) for b in range(NB)]
    cp_inv = pltpu.make_async_copy(inv_h, inv_v, lsem.at[6])
    cp_agg = pltpu.make_async_copy(agg_h, agg_v, lsem.at[7])
    cp_snd = pltpu.make_async_copy(snd_h, snd, lsem.at[8])
    cp_msk = pltpu.make_async_copy(msk_h, msk, lsem.at[9])
    cp_nbr = pltpu.make_async_copy(nbr_h, nbr, lsem.at[10])
    for cp in [cp_loads, cp_diag, cp_snd, cp_msk, cp_nbr] + cp_stiff + [cp_inv, cp_agg]:
        cp.start()

    def at(y_, zl_, core_, x_, zh_):
        return ((y_ * NZL + zl_) * 2 + core_, x_ * NZH + zh_)

    def g_peer(d):
        other = (g + d) % NG
        return at(y, zl, other // NX, other % NX, zh)

    def z_peer(d):
        other = (z + d) % NZ
        return at(y, other % NZL, core, x, other // NZL)

    def y_peer(d):
        return at((y + d) % NY, zl, core, x, zh)

    pending = []

    def rcopy(src, dst, ss, rs, dev):
        return pltpu.make_async_remote_copy(src_ref=src, dst_ref=dst, send_sem=ss, recv_sem=rs,
                                            device_id=dev, device_id_type=MESH)

    barrier = pltpu.get_barrier_semaphore()

    def greet(dev):
        pl.semaphore_signal(barrier, inc=1, device_id=dev, device_id_type=MESH)

    left_far = jnp.logical_and(core == 0, w > 0)
    right_far = jnp.logical_and(core == 1, w < N_WIDE - 1)
    pl.when(left_far)(lambda: greet((w - 1, n)))
    pl.when(right_far)(lambda: greet((w + 1, n)))
    for d in range(1, 8):
        greet(g_peer(d))
        greet(z_peer(d))
        greet(y_peer(d))

    @pl.when(w == 0)
    def _():
        ghost[:, 0:2] = jnp.zeros((3, 2, VEC, BS), F32)

    @pl.when(w == N_WIDE - 1)
    def _():
        ghost[:, 2:4] = jnp.zeros((3, 2, VEC, BS), F32)

    cp_loads.wait()
    cp_diag.wait()
    rdiag = [1.0 / diag_v[b:b + 1, :] for b in range(NB)]
    for b in range(NB):
        own[0, b] = loads_v[b] * rdiag[b]
    cp_snd.wait()

    def to_left(k):
        return rcopy(sbuf.at[k, pl.ds(0, 2)], ghost.at[k, pl.ds(2, 2)], halo_ss.at[k, 0], halo_rs.at[k, 0], (w - 1, n))

    def to_right(k):
        return rcopy(sbuf.at[k, pl.ds(2, 2)], ghost.at[k, pl.ds(0, 2)], halo_ss.at[k, 1], halo_rs.at[k, 1], (w + 1, n))

    def fill_halo(k):
        for j in range(4):
            sbuf[k, j] = own[k, snd[j]]

    def send_halo(k):
        pl.when(w > 0)(lambda: to_left(k).start())
        pl.when(w < N_WIDE - 1)(lambda: to_right(k).start())
        pending.append(lambda: pl.when(w > 0)(lambda: to_left(k).wait_send()))
        pending.append(lambda: pl.when(w < N_WIDE - 1)(lambda: to_right(k).wait_send()))

    def wait_halo(k):
        pl.when(w < N_WIDE - 1)(lambda: to_left(k).wait_recv())
        pl.when(w > 0)(lambda: to_right(k).wait_recv())

    fill_halo(0)

    @pl.when(jnp.logical_or(left_far, right_far))
    def _():
        pl.semaphore_wait(barrier, 22)

    @pl.when(jnp.logical_not(jnp.logical_or(left_far, right_far)))
    def _():
        pl.semaphore_wait(barrier, 21)

    send_halo(0)

    cp_msk.wait()
    ones = jnp.ones((16, BS), BF16)
    peak = None
    for b in range(NB):
        cp_stiff[b].wait()
        total = None
        for s in range(NS):
            block = stiff_v[b, s] * msk[b, s].astype(F32)
            size = jnp.abs(block)
            total = size if total is None else total + size
            block = block.T
            high = block.astype(BF16)
            w2[b, s * BS:(s + 1) * BS, 0:BS] = high
            w2[b, s * BS:(s + 1) * BS, BS:2 * BS] = (block - high.astype(F32)).astype(BF16)
        sums = dot(ones, split(total), NT)[:8]
        ratio = (sums[:, :BS] + sums[:, BS:]) / diag_v[b:b + 1, :]
        peak = ratio if peak is None else jnp.maximum(peak, ratio)
    mx[0, 0] = jnp.broadcast_to(jnp.max(peak, axis=1, keepdims=True), (8, BS))

    def peak_copy(stage, d):
        dev = (g_peer, z_peer, y_peer)[stage](d)
        row = pl.ds(0, 1)
        return rcopy(mx.at[stage, 0, row], mx.at[stage, d, row], mx_ss.at[stage, d], mx_rs.at[stage, d], dev)

    def send_peak(stage):
        for d in (4, 3, 5, 2, 6, 1, 7):
            peak_copy(stage, d).start()
            pending.append(peak_copy(stage, d).wait_send)

    def take_peak(stage):
        for d in range(1, 8):
            peak_copy(stage, d).wait_recv()
        top = mx[stage, 0, 0:1]
        for d in range(1, 8):
            top = jnp.maximum(top, mx[stage, d, 0:1])
        return top

    send_peak(0)

    def split_own(k):
        for b in range(NB):
            exts[b] = split(own[k, b])

    split_own(0)

    cp_inv.wait()
    for i in range(NY):
        for c in range(2):
            cols = [(NG * i + 2 * j + c) * BS for j in range(NZL)]
            for j, piece in enumerate(regroup([inv_v[:, col:col + BS] for col in cols], NX, 32)):
                inv_s[NX * c + j, i] = piece

    def inv_copy(d):
        other = (g + d) % NG
        return rcopy(inv_s.at[other], inv_r.at[g], inv_ss.at[d], inv_rs.at[d], g_peer(d))

    def send_inv(steps):
        for d in steps:
            inv_copy(d).start()
            pending.append(inv_copy(d).wait_send)

    send_inv((4, 1, 7))
    inv_r[g] = inv_s[g]
    cp_nbr.wait()

    def couple(k):
        wait_halo(k)
        for j in range(4):
            exts[NB + j] = split(ghost[k, j])
        for b in range(NB):
            fields = jnp.concatenate([exts[nbr[b, s]] for s in range(NS)], axis=1)
            coupled = folded(dot(fields, w2[b], NN))
            ksum[k, b] = coupled
            if k < SWEEPS:
                own[k + 1, b] = coupled * rdiag[b]
        if k < SWEEPS:
            fill_halo(k + 1)
            send_halo(k + 1)

    couple(0)
    mx[1, 0, 0:1] = take_peak(0)
    send_peak(1)
    send_inv((2, 6))
    split_own(1)

    cp_agg.wait()
    row = lax.broadcasted_iota(jnp.int32, (BS, BS), 0)
    turned = 32 * ((row // ROWS) % NX) + ROWS * (row // 64) + row % ROWS
    for b in range(NB):
        which = agg_v[b:b + 1, :]
        cols = slice(b * BS, (b + 1) * BS)
        oh[:, cols] = jnp.where(row == which, 1.0, 0.0).astype(BF16)
        ohs[:, cols] = jnp.where(turned == which, 1.0, 0.0).astype(BF16)

    couple(1)
    mx[2, 0, 0:1] = take_peak(1)
    send_peak(2)
    send_inv((3, 5))
    split_own(2)
    couple(2)
    upper = 1.0 + take_peak(2)

    centre = 0.625 * upper
    half_span = 0.375 * upper
    spread_ratio = 5.0 / 3.0
    weight_prev = 0.6
    zero = jnp.zeros_like(upper)
    delta = [1.0 / centre, zero, zero]
    sigma = list(delta)
    rho = [zero + 1.0, zero, zero, zero]

    def apply(rho, delta):
        rho = list(rho)
        for j in range(3):
            rho[j] = rho[j] - delta[j]
            rho[j + 1] = rho[j + 1] + delta[j]
        return rho

    for _ in range(SWEEPS):
        rho = apply(rho, delta)
        weight = 1.0 / (2.0 * spread_ratio - weight_prev)
        gain = 2.0 * weight / half_span
        delta = [weight * weight_prev * delta[j] + gain * rho[j] for j in range(3)]
        sigma = [sigma[j] + delta[j] for j in range(3)]
        weight_prev = weight
    rho = apply(rho, delta)

    parts = []
    for b in range(NB):
        residual = rho[0] * loads_v[b] + rho[1] * ksum[0, b] + rho[2] * ksum[1, b] + rho[3] * ksum[2, b]
        res_v[b] = residual
        parts.append(split(residual))
    pair = dot(jnp.concatenate(parts, axis=1), oh[...], NT)
    part = pair[:VEC] + pair[VEC:]

    for j, piece in enumerate(regroup([part[8 * i:8 * i + 8] for i in range(3)], NX, 32)):
        i_s[j] = piece
    side = NX * zh + x
    i_r[zl, side] = i_s[x]
    plane = [(dx, dz) for dx in range(NX) for dz in range(NZ) if dx or dz]
    plane.sort(key=lambda p: -hops(p[0], NX) - hops(p[1], NZ))

    def i_copy(dx, dz):
        other = (z + dz) % NZ
        ox = (x + dx) % NX
        k = NZ * dx + dz
        return rcopy(i_s.at[ox], i_r.at[zl, side], i_ss.at[k], i_rs.at[k],
                     at(y, other % NZL, core, ox, other // NZL))

    def i_arrival(dx, dz):
        came = (z + NZ - dz) % NZ
        cx = (x + NX - dx) % NX
        k = NZ * dx + dz
        slot = i_r.at[came % NZL, NX * (came // NZL) + cx]
        return rcopy(slot, slot, i_ss.at[k], i_rs.at[k], z_peer(1))

    for dx, dz in plane:
        i_copy(dx, dz).start()
        pending.append(i_copy(dx, dz).wait_send)

    for b in range(NB):
        corr_v[b] = sigma[0] * own[0, b] + sigma[1] * own[1, b] + sigma[2] * own[2, b]
    for d in range(1, NG):
        inv_copy(d).wait_recv()
    for j in range(NG):
        for i in range(NY):
            block = inv_r[j, i]
            high = block.astype(BF16)
            cols = slice(i * BS, (i + 1) * BS)
            wc[j * ROWS:(j + 1) * ROWS, cols] = high
            wc[BS + j * ROWS:BS + (j + 1) * ROWS, cols] = (block - high.astype(F32)).astype(BF16)

    for dx, dz in reversed(plane):
        i_arrival(dx, dz).wait_recv()
    tiles = []
    for j in range(NZL):
        total = i_r[j, 0]
        for k in range(1, 2 * NX):
            total = total + i_r[j, k]
        tiles.append(total)
    c_r[y] = jnp.concatenate(regroup(tiles, 3, 32), axis=0)

    def c_copy(d):
        return rcopy(c_r.at[y], c_r.at[y], c_ss.at[d], c_rs.at[d], y_peer(d))

    def c_arrival(d):
        came = (y - d + NY) % NY
        return rcopy(c_r.at[came], c_r.at[came], c_ss.at[d], c_rs.at[d], y_peer(d))

    for d in (4, 3, 5, 2, 6, 1, 7):
        c_copy(d).start()
        pending.append(c_copy(d).wait_send)
    for d in (1, 7, 2, 6, 3, 5, 4):
        c_arrival(d).wait_recv()
    fields = jnp.concatenate([split(c_r[i]) for i in range(NY)], axis=1)
    coarse = folded(dot(fields, wc[...], NT))

    low = lax.broadcasted_iota(jnp.int32, (8, BS), 1) < 64
    t0, t1, t2 = coarse[0:8], coarse[8:16], coarse[16:24]
    u0, u1, u2 = roll(t0, 64), roll(t1, 64), roll(t2, 64)
    d_s[0] = jnp.concatenate([jnp.where(low, t0, u1), jnp.where(low[:4], t2[0:4], u2[4:8])], axis=0)
    d_s[1] = jnp.concatenate([jnp.where(low, u0, t1), jnp.where(low[:4], u2[0:4], t2[4:8])], axis=0)
    d_r[zh, g] = d_s[core]
    around = [(dg, dh) for dg in range(NG) for dh in range(NZH) if dg or dh]
    around.sort(key=lambda p: -4 * p[1] - hops(p[0], NG))

    def d_copy(dg, dh):
        other = (g + dg) % NG
        k = NG * dh + dg
        return rcopy(d_s.at[other // NX], d_r.at[zh, g], d_ss.at[k], d_rs.at[k],
                     at(y, zl, other // NX, other % NX, (zh + dh) % NZH))

    def d_arrival(dg, dh):
        slot = d_r.at[(zh + dh) % NZH, (g + NG - dg) % NG]
        k = NG * dh + dg
        return rcopy(slot, slot, d_ss.at[k], d_rs.at[k], z_peer(1))

    for dg, dh in around:
        d_copy(dg, dh).start()
        pending.append(d_copy(dg, dh).wait_send)
    for wait in pending:
        wait()
    for dg, dh in reversed(around):
        d_arrival(dg, dh).wait_recv()
    sums = []
    for h in range(NZH):
        total = d_r[h, 0]
        for j in range(1, NG):
            total = total + d_r[h, j]
        sums.append(total)

    def tail(value):
        return jnp.concatenate([value[8:12], roll(value[8:12], 64)], axis=0)

    p0, p1 = sums[0][:8], sums[1][:8]
    q0, q1 = tail(sums[0]), tail(sums[1])
    solved = jnp.concatenate([jnp.where(low, p0, roll(p1, 64)), jnp.where(low, roll(p0, 64), p1),
                              jnp.where(low, q0, roll(q1, 64))], axis=0)
    pair = dot(split(solved), ohs[...], NN)
    for b in range(NB):
        cols = slice(b * BS, (b + 1) * BS)
        corr_v[b] = corr_v[b] + (pair[:VEC, cols] + pair[VEC:, cols])


def shards(loads, diagonal, stiffness, neighbors, slot_mask, send_list, aggregate, coarse_inverse):
    hbm = pl.BlockSpec(memory_space=pltpu.HBM)
    vmem = pl.BlockSpec(memory_space=pltpu.VMEM)
    field = (NB, VEC, BS)
    dma = pltpu.SemaphoreType.DMA
    corr, res = pl.pallas_call(
        kernel,
        out_shape=(pltpu.VMEM(field, F32), pltpu.VMEM(field, F32)),
        in_specs=[hbm] * 8,
        out_specs=(vmem, vmem),
        scratch_shapes=[
            pltpu.SMEM((NB, NS), jnp.int32),
            pltpu.SMEM((NB, NS), jnp.int32),
            pltpu.SMEM((4,), jnp.int32),
            pltpu.VMEM(field, F32),
            pltpu.VMEM((NB, BS), F32),
            pltpu.VMEM((NB, NS, BS, BS), F32),
            pltpu.VMEM((NB, BS), jnp.int32),
            pltpu.VMEM((ROWS, NG * NY * BS), F32),
            pltpu.VMEM((3,) + field, F32),
            pltpu.VMEM((3,) + field, F32),
            pltpu.VMEM((3,) + field, F32),
            pltpu.VMEM((3,) + field, F32),
            pltpu.VMEM((2 * NB, 2 * VEC, BS), BF16),
            pltpu.VMEM((NB, NS * BS, 2 * BS), BF16),
            pltpu.VMEM((3, 8, 8, BS), F32),
            pltpu.VMEM((NG, NY, ROWS, BS), F32),
            pltpu.VMEM((NG, NY, ROWS, BS), F32),
            pltpu.VMEM((2 * BS, NY * BS), BF16),
            pltpu.VMEM((BS, NB * BS), BF16),
            pltpu.VMEM((BS, NB * BS), BF16),
            pltpu.VMEM((NX, 8, BS), F32),
            pltpu.VMEM((NZL, 2 * NX, 8, BS), F32),
            pltpu.VMEM((NY, VEC, BS), F32),
            pltpu.VMEM((2, 12, BS), F32),
            pltpu.VMEM((NZH, NG, 12, BS), F32),
            dma((11,)),
            dma((3, 2)), dma((3, 2)),
            dma((3, 8)), dma((3, 8)),
            dma((8,)), dma((8,)),
            dma((32,)), dma((32,)),
            dma((8,)), dma((8,)),
            dma((16,)), dma((16,)),
        ],
        compiler_params=pltpu.CompilerParams(collective_id=0, has_side_effects=True, vmem_limit_bytes=58 * 1024 * 1024),
    )(neighbors, slot_mask, send_list, loads, diagonal, stiffness, aggregate, coarse_inverse)
    return corr, res


def solution(mesh):
    both = ("wide", "narrow")
    return jax.shard_map(
        shards,
        mesh=mesh,
        in_specs=(
            P(both, None, None),
            P(both, None),
            P(both, None, None, None),
            P(both, None),
            P(both, None),
            P(both),
            P(both, None),
            P(both, None),
        ),
        out_specs=(P(both, None, None), P(both, None, None)),
        check_vma=False,
    )
```

```python
import jax
import jax.numpy as jnp
from jax import lax
from jax.experimental import pallas as pl
from jax.experimental.pallas import tpu as pltpu
from jax.sharding import PartitionSpec as P

F32 = jnp.float32
BF16 = jnp.bfloat16
MESH = pl.DeviceIdType.MESH
NB, NS, VEC, BS = 4, 4, 24, 128
NX, NY, NZL, NZH = 4, 8, 4, 2
NZ = NZL * NZH
NG = 2 * NX
N_WIDE = NY * NZL * 2
SWEEPS = 2
ROWS = 16
NT = (((1,), (1,)), ((), ()))
NN = (((1,), (0,)), ((), ()))


def split(value):
    high = value.astype(BF16).astype(F32)
    return jnp.concatenate([high, value - high], axis=0).astype(BF16)


def dot(a, b, dims):
    return lax.dot_general(a, b, dims, preferred_element_type=F32)


def folded(full):
    half = full.shape[0] // 2
    cols = full.shape[1] // 2
    return full[:half, :cols] + (full[:half, cols:] + full[half:, :cols])


def roll(value, lanes):
    return value if lanes % BS == 0 else pltpu.roll(value, lanes % BS, 1)


def regroup(tiles, count, width):
    lane = lax.broadcasted_iota(jnp.int32, tiles[0].shape, 1) // width
    out = []
    for i in range(count):
        acc = None
        for j, tile in enumerate(tiles):
            moved = roll(tile, width * (j - i))
            acc = moved if acc is None else jnp.where(lane == j, moved, acc)
        out.append(acc)
    return out


def mod(value, size):
    return lax.rem(value, jnp.int32(size))


def div(value, size):
    return lax.div(value, jnp.int32(size))


def hops(step, size):
    return min(step, size - step)


def kernel(nbr_h, msk_h, snd_h, loads_h, diag_h, stiff_h, agg_h, inv_h, corr_v, res_v,
           nbr, msk, snd, loads_v, diag_v, stiff_v, agg_v, inv_v, own, ksum, sbuf, ghost, exts, w2,
           mx, inv_s, inv_r, wc, oh, ohs, i_s, i_r, c_r, d_s, d_r,
           lsem, halo_ss, halo_rs, mx_ss, mx_rs, inv_ss, inv_rs, i_ss, i_rs, c_ss, c_rs, d_ss, d_rs):
    w = lax.axis_index("wide")
    n = lax.axis_index("narrow")
    core = mod(w, 2)
    zl = mod(div(w, 2), NZL)
    y = div(w, 2 * NZL)
    x = div(n, NZH)
    zh = mod(n, NZH)
    z = zh * NZL + zl
    g = NX * core + x

    cp_loads = pltpu.make_async_copy(loads_h, loads_v, lsem.at[0])
    cp_diag = pltpu.make_async_copy(diag_h, diag_v, lsem.at[1])
    cp_stiff = [pltpu.make_async_copy(stiff_h.at[b], stiff_v.at[b], lsem.at[2 + b]) for b in range(NB)]
    cp_inv = pltpu.make_async_copy(inv_h, inv_v, lsem.at[6])
    cp_agg = pltpu.make_async_copy(agg_h, agg_v, lsem.at[7])
    cp_snd = pltpu.make_async_copy(snd_h, snd, lsem.at[8])
    cp_msk = pltpu.make_async_copy(msk_h, msk, lsem.at[9])
    cp_nbr = pltpu.make_async_copy(nbr_h, nbr, lsem.at[10])
    for cp in [cp_loads, cp_diag, cp_snd, cp_msk, cp_nbr] + cp_stiff + [cp_inv, cp_agg]:
        cp.start()

    def at(y_, zl_, core_, x_, zh_):
        return ((y_ * NZL + zl_) * 2 + core_, x_ * NZH + zh_)

    def g_peer(d):
        other = mod(g + d, NG)
        return at(y, zl, div(other, NX), mod(other, NX), zh)

    def z_peer(d):
        other = mod(z + d, NZ)
        return at(y, mod(other, NZL), core, x, div(other, NZL))

    def y_peer(d):
        return at(mod(y + d, NY), zl, core, x, zh)

    pending = []

    def rcopy(src, dst, ss, rs, dev):
        return pltpu.make_async_remote_copy(src_ref=src, dst_ref=dst, send_sem=ss, recv_sem=rs,
                                            device_id=dev, device_id_type=MESH)

    barrier = pltpu.get_barrier_semaphore()

    def greet(dev):
        pl.semaphore_signal(barrier, inc=1, device_id=dev, device_id_type=MESH)

    left_far = jnp.logical_and(core == 0, w > 0)
    right_far = jnp.logical_and(core == 1, w < N_WIDE - 1)
    pl.when(left_far)(lambda: greet((w - 1, n)))
    pl.when(right_far)(lambda: greet((w + 1, n)))
    for d in range(1, 8):
        greet(g_peer(d))
        greet(z_peer(d))
        greet(y_peer(d))

    @pl.when(w == 0)
    def _():
        ghost[:, 0:2] = jnp.zeros((3, 2, VEC, BS), F32)

    @pl.when(w == N_WIDE - 1)
    def _():
        ghost[:, 2:4] = jnp.zeros((3, 2, VEC, BS), F32)

    cp_loads.wait()
    cp_diag.wait()
    rdiag = [1.0 / diag_v[b:b + 1, :] for b in range(NB)]
    for b in range(NB):
        own[0, b] = loads_v[b] * rdiag[b]
    cp_snd.wait()

    def to_left(k):
        return rcopy(sbuf.at[k, pl.ds(0, 2)], ghost.at[k, pl.ds(2, 2)], halo_ss.at[k, 0], halo_rs.at[k, 0], (w - 1, n))

    def to_right(k):
        return rcopy(sbuf.at[k, pl.ds(2, 2)], ghost.at[k, pl.ds(0, 2)], halo_ss.at[k, 1], halo_rs.at[k, 1], (w + 1, n))

    def fill_halo(k):
        for j in range(4):
            sbuf[k, j] = own[k, snd[j]]

    def send_halo(k):
        pl.when(w > 0)(lambda: to_left(k).start())
        pl.when(w < N_WIDE - 1)(lambda: to_right(k).start())
        pending.append(lambda: pl.when(w > 0)(lambda: to_left(k).wait_send()))
        pending.append(lambda: pl.when(w < N_WIDE - 1)(lambda: to_right(k).wait_send()))

    def wait_halo(k):
        pl.when(w < N_WIDE - 1)(lambda: to_left(k).wait_recv())
        pl.when(w > 0)(lambda: to_right(k).wait_recv())

    fill_halo(0)

    @pl.when(jnp.logical_or(left_far, right_far))
    def _():
        pl.semaphore_wait(barrier, 22)

    @pl.when(jnp.logical_not(jnp.logical_or(left_far, right_far)))
    def _():
        pl.semaphore_wait(barrier, 21)

    send_halo(0)

    cp_msk.wait()
    ones = jnp.ones((16, BS), BF16)
    peak = None
    for b in range(NB):
        cp_stiff[b].wait()
        total = None
        for s in range(NS):
            block = stiff_v[b, s] * msk[b, s].astype(F32)
            size = jnp.abs(block)
            total = size if total is None else total + size
            block = block.T
            high = block.astype(BF16)
            w2[b, s * BS:(s + 1) * BS, 0:BS] = high
            w2[b, s * BS:(s + 1) * BS, BS:2 * BS] = (block - high.astype(F32)).astype(BF16)
        sums = dot(ones, split(total), NT)[:8]
        ratio = (sums[:, :BS] + sums[:, BS:]) / diag_v[b:b + 1, :]
        peak = ratio if peak is None else jnp.maximum(peak, ratio)
    mx[0, 0] = jnp.broadcast_to(jnp.max(peak, axis=1, keepdims=True), (8, BS))

    def peak_copy(stage, d):
        dev = (g_peer, z_peer, y_peer)[stage](d)
        row = pl.ds(0, 1)
        return rcopy(mx.at[stage, 0, row], mx.at[stage, d, row], mx_ss.at[stage, d], mx_rs.at[stage, d], dev)

    def send_peak(stage):
        for d in (4, 3, 5, 2, 6, 1, 7):
            peak_copy(stage, d).start()
            pending.append(peak_copy(stage, d).wait_send)

    def take_peak(stage):
        for d in range(1, 8):
            peak_copy(stage, d).wait_recv()
        top = mx[stage, 0, 0:1]
        for d in range(1, 8):
            top = jnp.maximum(top, mx[stage, d, 0:1])
        return top

    send_peak(0)

    def split_own(k):
        for b in range(NB):
            exts[b] = split(own[k, b])

    split_own(0)

    cp_inv.wait()
    for i in range(NY):
        for c in range(2):
            cols = [(NG * i + 2 * j + c) * BS for j in range(NZL)]
            for j, piece in enumerate(regroup([inv_v[:, col:col + BS] for col in cols], NX, 32)):
                inv_s[NX * c + j, i] = piece

    def inv_copy(d):
        other = mod(g + d, NG)
        return rcopy(inv_s.at[other], inv_r.at[g], inv_ss.at[d], inv_rs.at[d], g_peer(d))

    def send_inv(steps):
        for d in steps:
            inv_copy(d).start()
            pending.append(inv_copy(d).wait_send)

    send_inv((4, 1, 7))
    inv_r[g] = inv_s[g]
    cp_nbr.wait()

    def couple(k):
        wait_halo(k)
        for j in range(4):
            exts[NB + j] = split(ghost[k, j])
        for b in range(NB):
            fields = jnp.concatenate([exts[nbr[b, s]] for s in range(NS)], axis=1)
            coupled = folded(dot(fields, w2[b], NN))
            ksum[k, b] = coupled
            if k < SWEEPS:
                own[k + 1, b] = coupled * rdiag[b]
        if k < SWEEPS:
            fill_halo(k + 1)
            send_halo(k + 1)

    couple(0)
    mx[1, 0, 0:1] = take_peak(0)
    send_peak(1)
    send_inv((2, 6))
    split_own(1)

    cp_agg.wait()
    row = lax.broadcasted_iota(jnp.int32, (BS, BS), 0)
    turned = 32 * ((row // ROWS) % NX) + ROWS * (row // 64) + row % ROWS
    for b in range(NB):
        which = agg_v[b:b + 1, :]
        cols = slice(b * BS, (b + 1) * BS)
        oh[:, cols] = jnp.where(row == which, 1.0, 0.0).astype(BF16)
        ohs[:, cols] = jnp.where(turned == which, 1.0, 0.0).astype(BF16)

    def pass_peak(stage):
        mx[stage, 0, 0:1] = take_peak(stage - 1)
        for d in (4, 3, 5, 2, 6, 1, 7):
            peak_copy(stage, d).start()

    turn = jnp.logical_or(jnp.logical_and(core == 0, zl == 0), jnp.logical_and(core == 1, zl == NZL - 1))
    pl.when(turn)(lambda: pass_peak(2))
    couple(1)
    pl.when(jnp.logical_not(turn))(lambda: pass_peak(2))
    pending.extend(peak_copy(2, d).wait_send for d in range(1, 8))
    send_inv((3, 5))
    split_own(2)
    couple(2)
    upper = 1.0 + take_peak(2)

    centre = 0.625 * upper
    half_span = 0.375 * upper
    spread_ratio = 5.0 / 3.0
    weight_prev = 0.6
    zero = jnp.zeros_like(upper)
    delta = [1.0 / centre, zero, zero]
    sigma = list(delta)
    rho = [zero + 1.0, zero, zero, zero]

    def apply(rho, delta):
        rho = list(rho)
        for j in range(3):
            rho[j] = rho[j] - delta[j]
            rho[j + 1] = rho[j + 1] + delta[j]
        return rho

    for _ in range(SWEEPS):
        rho = apply(rho, delta)
        weight = 1.0 / (2.0 * spread_ratio - weight_prev)
        gain = 2.0 * weight / half_span
        delta = [weight * weight_prev * delta[j] + gain * rho[j] for j in range(3)]
        sigma = [sigma[j] + delta[j] for j in range(3)]
        weight_prev = weight
    rho = apply(rho, delta)

    parts = []
    for b in range(NB):
        residual = rho[0] * loads_v[b] + rho[1] * ksum[0, b] + rho[2] * ksum[1, b] + rho[3] * ksum[2, b]
        res_v[b] = residual
        parts.append(split(residual))
    pair = dot(jnp.concatenate(parts, axis=1), oh[...], NT)
    part = pair[:VEC] + pair[VEC:]

    for j, piece in enumerate(regroup([part[8 * i:8 * i + 8] for i in range(3)], NX, 32)):
        i_s[j] = piece
    side = NX * zh + x
    i_r[zl, side] = i_s[x]
    plane = [(dx, dz) for dx in range(NX) for dz in range(NZ) if dx or dz]
    plane.sort(key=lambda p: -hops(p[0], NX) - hops(p[1], NZ))

    def i_copy(dx, dz):
        other = mod(z + dz, NZ)
        ox = mod(x + dx, NX)
        k = NZ * dx + dz
        return rcopy(i_s.at[ox], i_r.at[zl, side], i_ss.at[k], i_rs.at[k],
                     at(y, mod(other, NZL), core, ox, div(other, NZL)))

    def i_arrival(dx, dz):
        came = mod(z + NZ - dz, NZ)
        cx = mod(x + NX - dx, NX)
        k = NZ * dx + dz
        slot = i_r.at[mod(came, NZL), NX * div(came, NZL) + cx]
        return rcopy(slot, slot, i_ss.at[k], i_rs.at[k], z_peer(1))

    for dx, dz in plane:
        i_copy(dx, dz).start()
        pending.append(i_copy(dx, dz).wait_send)

    for b in range(NB):
        corr_v[b] = sigma[0] * own[0, b] + sigma[1] * own[1, b] + sigma[2] * own[2, b]
    for d in range(1, NG):
        inv_copy(d).wait_recv()
    for i in range(NY):
        block = jnp.concatenate([inv_r[j, i] for j in range(NG)], axis=0).T
        high = block.astype(BF16)
        rows = slice(i * BS, (i + 1) * BS)
        wc[rows, 0:BS] = high
        wc[rows, BS:2 * BS] = (block - high.astype(F32)).astype(BF16)

    for dx, dz in reversed(plane):
        i_arrival(dx, dz).wait_recv()
    tiles = []
    for j in range(NZL):
        total = i_r[j, 0]
        for k in range(1, 2 * NX):
            total = total + i_r[j, k]
        tiles.append(total)
    c_r[y] = jnp.concatenate(regroup(tiles, 3, 32), axis=0)

    def c_copy(d):
        return rcopy(c_r.at[y], c_r.at[y], c_ss.at[d], c_rs.at[d], y_peer(d))

    def c_arrival(d):
        came = mod(y - d + NY, NY)
        return rcopy(c_r.at[came], c_r.at[came], c_ss.at[d], c_rs.at[d], y_peer(d))

    for d in (4, 3, 5, 2, 6, 1, 7):
        c_copy(d).start()
        pending.append(c_copy(d).wait_send)
    for d in (1, 7, 2, 6, 3, 5, 4):
        c_arrival(d).wait_recv()
    fields = jnp.concatenate([split(c_r[i]) for i in range(NY)], axis=1)
    coarse = folded(dot(fields, wc[...], NN))

    low = lax.broadcasted_iota(jnp.int32, (8, BS), 1) < 64
    t0, t1, t2 = coarse[0:8], coarse[8:16], coarse[16:24]
    u0, u1, u2 = roll(t0, 64), roll(t1, 64), roll(t2, 64)
    d_s[0] = jnp.concatenate([jnp.where(low, t0, u1), jnp.where(low[:4], t2[0:4], u2[4:8])], axis=0)
    d_s[1] = jnp.concatenate([jnp.where(low, u0, t1), jnp.where(low[:4], u2[0:4], t2[4:8])], axis=0)
    d_r[zh, g] = d_s[core]
    around = [(dg, dh) for dg in range(NG) for dh in range(NZH) if dg or dh]
    around.sort(key=lambda p: -4 * p[1] - hops(p[0], NG))

    def d_copy(dg, dh):
        other = mod(g + dg, NG)
        k = NG * dh + dg
        return rcopy(d_s.at[div(other, NX)], d_r.at[zh, g], d_ss.at[k], d_rs.at[k],
                     at(y, zl, div(other, NX), mod(other, NX), mod(zh + dh, NZH)))

    def d_arrival(dg, dh):
        slot = d_r.at[mod(zh + dh, NZH), mod(g + NG - dg, NG)]
        k = NG * dh + dg
        return rcopy(slot, slot, d_ss.at[k], d_rs.at[k], z_peer(1))

    for dg, dh in around:
        d_copy(dg, dh).start()
        pending.append(d_copy(dg, dh).wait_send)
    for wait in pending:
        wait()
    for dg, dh in reversed(around):
        d_arrival(dg, dh).wait_recv()
    sums = []
    for h in range(NZH):
        total = d_r[h, 0]
        for j in range(1, NG):
            total = total + d_r[h, j]
        sums.append(total)

    def tail(value):
        return jnp.concatenate([value[8:12], roll(value[8:12], 64)], axis=0)

    p0, p1 = sums[0][:8], sums[1][:8]
    q0, q1 = tail(sums[0]), tail(sums[1])
    solved = jnp.concatenate([jnp.where(low, p0, roll(p1, 64)), jnp.where(low, roll(p0, 64), p1),
                              jnp.where(low, q0, roll(q1, 64))], axis=0)
    pair = dot(split(solved), ohs[...], NN)
    for b in range(NB):
        cols = slice(b * BS, (b + 1) * BS)
        corr_v[b] = corr_v[b] + (pair[:VEC, cols] + pair[VEC:, cols])


def store(corr_v, res_v, corr_h, res_h, sem):
    one = pltpu.make_async_copy(corr_v, corr_h, sem.at[0])
    two = pltpu.make_async_copy(res_v, res_h, sem.at[1])
    one.start()
    two.start()
    one.wait()
    two.wait()


def shards(loads, diagonal, stiffness, neighbors, slot_mask, send_list, aggregate, coarse_inverse):
    hbm = pl.BlockSpec(memory_space=pltpu.HBM)
    vmem = pl.BlockSpec(memory_space=pltpu.VMEM)
    field = (NB, VEC, BS)
    dma = pltpu.SemaphoreType.DMA
    corr, res = pl.pallas_call(
        kernel,
        out_shape=(pltpu.VMEM(field, F32), pltpu.VMEM(field, F32)),
        in_specs=[hbm] * 8,
        out_specs=(vmem, vmem),
        scratch_shapes=[
            pltpu.SMEM((NB, NS), jnp.int32),
            pltpu.SMEM((NB, NS), jnp.int32),
            pltpu.SMEM((4,), jnp.int32),
            pltpu.VMEM(field, F32),
            pltpu.VMEM((NB, BS), F32),
            pltpu.VMEM((NB, NS, BS, BS), F32),
            pltpu.VMEM((NB, BS), jnp.int32),
            pltpu.VMEM((ROWS, NG * NY * BS), F32),
            pltpu.VMEM((3,) + field, F32),
            pltpu.VMEM((3,) + field, F32),
            pltpu.VMEM((3,) + field, F32),
            pltpu.VMEM((3,) + field, F32),
            pltpu.VMEM((2 * NB, 2 * VEC, BS), BF16),
            pltpu.VMEM((NB, NS * BS, 2 * BS), BF16),
            pltpu.VMEM((3, 8, 8, BS), F32),
            pltpu.VMEM((NG, NY, ROWS, BS), F32),
            pltpu.VMEM((NG, NY, ROWS, BS), F32),
            pltpu.VMEM((NY * BS, 2 * BS), BF16),
            pltpu.VMEM((BS, NB * BS), BF16),
            pltpu.VMEM((BS, NB * BS), BF16),
            pltpu.VMEM((NX, 8, BS), F32),
            pltpu.VMEM((NZL, 2 * NX, 8, BS), F32),
            pltpu.VMEM((NY, VEC, BS), F32),
            pltpu.VMEM((2, 12, BS), F32),
            pltpu.VMEM((NZH, NG, 12, BS), F32),
            dma((11,)),
            dma((3, 2)), dma((3, 2)),
            dma((3, 8)), dma((3, 8)),
            dma((8,)), dma((8,)),
            dma((32,)), dma((32,)),
            dma((8,)), dma((8,)),
            dma((16,)), dma((16,)),
        ],
        compiler_params=pltpu.CompilerParams(collective_id=0, has_side_effects=True, vmem_limit_bytes=58 * 1024 * 1024),
    )(neighbors, slot_mask, send_list, loads, diagonal, stiffness, aggregate, coarse_inverse)
    corr = pltpu.with_memory_space_constraint(corr, pltpu.VMEM)
    res = pltpu.with_memory_space_constraint(res, pltpu.VMEM)
    return pl.pallas_call(
        store,
        out_shape=(jax.ShapeDtypeStruct(field, F32), jax.ShapeDtypeStruct(field, F32)),
        in_specs=[vmem, vmem],
        out_specs=(hbm, hbm),
        scratch_shapes=[dma((2,))],
    )(corr, res)


def solution(mesh):
    both = ("wide", "narrow")
    return jax.shard_map(
        shards,
        mesh=mesh,
        in_specs=(
            P(both, None, None),
            P(both, None),
            P(both, None, None, None),
            P(both, None),
            P(both, None),
            P(both),
            P(both, None),
            P(both, None),
        ),
        out_specs=(P(both, None, None), P(both, None, None)),
        check_vma=False,
    )
```

```python
import jax
import jax.numpy as jnp
from jax import lax
from jax.experimental import pallas as pl
from jax.experimental.pallas import tpu as pltpu
from jax.sharding import PartitionSpec as P

F32 = jnp.float32
BF16 = jnp.bfloat16
MESH = pl.DeviceIdType.MESH
NB, NS, VEC, BS = 4, 4, 24, 128
NX, NY, NZL, NZH = 4, 8, 4, 2
NZ = NZL * NZH
NG = 2 * NX
N_WIDE = NY * NZL * 2
SWEEPS = 2
ROWS = 16
NT = (((1,), (1,)), ((), ()))
NN = (((1,), (0,)), ((), ()))


def split(value):
    high = value.astype(BF16).astype(F32)
    return jnp.concatenate([high, value - high], axis=0).astype(BF16)


def dot(a, b, dims):
    return lax.dot_general(a, b, dims, preferred_element_type=F32)


def folded(full):
    half = full.shape[0] // 2
    cols = full.shape[1] // 2
    return full[:half, :cols] + (full[:half, cols:] + full[half:, :cols])


def roll(value, lanes):
    return value if lanes % BS == 0 else pltpu.roll(value, lanes % BS, 1)


def regroup(tiles, count, width):
    lane = lax.broadcasted_iota(jnp.int32, tiles[0].shape, 1) // width
    out = []
    for i in range(count):
        acc = None
        for j, tile in enumerate(tiles):
            moved = roll(tile, width * (j - i))
            acc = moved if acc is None else jnp.where(lane == j, moved, acc)
        out.append(acc)
    return out


def mod(value, size):
    return lax.rem(value, jnp.int32(size))


def div(value, size):
    return lax.div(value, jnp.int32(size))


def hops(step, size):
    return min(step, size - step)


def kernel(nbr_h, msk_h, snd_h, loads_h, diag_h, stiff_h, agg_h, inv_h, corr_v, res_v,
           nbr, msk, snd, loads_v, diag_v, stiff_v, agg_v, inv_v, own, ksum, sbuf, ghost, exts, w2,
           mx, inv_s, inv_r, wc, oh, ohs, i_s, i_r, c_r, d_s, d_r,
           lsem, halo_ss, halo_rs, mx_ss, mx_rs, inv_ss, inv_rs, i_ss, i_rs, c_ss, c_rs, d_ss, d_rs):
    w = lax.axis_index("wide")
    n = lax.axis_index("narrow")
    core = mod(w, 2)
    zl = mod(div(w, 2), NZL)
    y = div(w, 2 * NZL)
    x = div(n, NZH)
    zh = mod(n, NZH)
    z = zh * NZL + zl
    g = NX * core + x

    cp_loads = pltpu.make_async_copy(loads_h, loads_v, lsem.at[0])
    cp_diag = pltpu.make_async_copy(diag_h, diag_v, lsem.at[1])
    cp_stiff = [pltpu.make_async_copy(stiff_h.at[b], stiff_v.at[b], lsem.at[2 + b]) for b in range(NB)]
    cp_inv = pltpu.make_async_copy(inv_h, inv_v, lsem.at[6])
    cp_agg = pltpu.make_async_copy(agg_h, agg_v, lsem.at[7])
    cp_snd = pltpu.make_async_copy(snd_h, snd, lsem.at[8])
    cp_msk = pltpu.make_async_copy(msk_h, msk, lsem.at[9])
    cp_nbr = pltpu.make_async_copy(nbr_h, nbr, lsem.at[10])
    for cp in [cp_loads, cp_diag, cp_snd, cp_msk, cp_nbr] + cp_stiff + [cp_inv, cp_agg]:
        cp.start()

    def at(y_, zl_, core_, x_, zh_):
        return ((y_ * NZL + zl_) * 2 + core_, x_ * NZH + zh_)

    def g_peer(d):
        other = mod(g + d, NG)
        return at(y, zl, div(other, NX), mod(other, NX), zh)

    def z_peer(d):
        other = mod(z + d, NZ)
        return at(y, mod(other, NZL), core, x, div(other, NZL))

    def y_peer(d):
        return at(mod(y + d, NY), zl, core, x, zh)

    pending = []

    def rcopy(src, dst, ss, rs, dev):
        return pltpu.make_async_remote_copy(src_ref=src, dst_ref=dst, send_sem=ss, recv_sem=rs,
                                            device_id=dev, device_id_type=MESH)

    barrier = pltpu.get_barrier_semaphore()

    def greet(dev):
        pl.semaphore_signal(barrier, inc=1, device_id=dev, device_id_type=MESH)

    left_far = jnp.logical_and(core == 0, w > 0)
    right_far = jnp.logical_and(core == 1, w < N_WIDE - 1)
    pl.when(left_far)(lambda: greet((w - 1, n)))
    pl.when(right_far)(lambda: greet((w + 1, n)))
    for d in range(1, 8):
        greet(g_peer(d))
        greet(z_peer(d))
        greet(y_peer(d))

    @pl.when(w == 0)
    def _():
        ghost[:, 0:2] = jnp.zeros((3, 2, VEC, BS), F32)

    @pl.when(w == N_WIDE - 1)
    def _():
        ghost[:, 2:4] = jnp.zeros((3, 2, VEC, BS), F32)

    cp_loads.wait()
    cp_diag.wait()
    rdiag = [1.0 / diag_v[b:b + 1, :] for b in range(NB)]
    for b in range(NB):
        own[0, b] = loads_v[b] * rdiag[b]
    cp_snd.wait()

    def to_left(k):
        return rcopy(sbuf.at[k, pl.ds(0, 2)], ghost.at[k, pl.ds(2, 2)], halo_ss.at[k, 0], halo_rs.at[k, 0], (w - 1, n))

    def to_right(k):
        return rcopy(sbuf.at[k, pl.ds(2, 2)], ghost.at[k, pl.ds(0, 2)], halo_ss.at[k, 1], halo_rs.at[k, 1], (w + 1, n))

    def fill_halo(k):
        for j in range(4):
            sbuf[k, j] = own[k, snd[j]]

    def send_halo(k):
        pl.when(w > 0)(lambda: to_left(k).start())
        pl.when(w < N_WIDE - 1)(lambda: to_right(k).start())
        pending.append(lambda: pl.when(w > 0)(lambda: to_left(k).wait_send()))
        pending.append(lambda: pl.when(w < N_WIDE - 1)(lambda: to_right(k).wait_send()))

    def wait_halo(k):
        pl.when(w < N_WIDE - 1)(lambda: to_left(k).wait_recv())
        pl.when(w > 0)(lambda: to_right(k).wait_recv())

    fill_halo(0)

    @pl.when(jnp.logical_or(left_far, right_far))
    def _():
        pl.semaphore_wait(barrier, 22)

    @pl.when(jnp.logical_not(jnp.logical_or(left_far, right_far)))
    def _():
        pl.semaphore_wait(barrier, 21)

    send_halo(0)

    cp_msk.wait()
    ones = jnp.ones((16, BS), BF16)
    mask = [[msk[b, s].astype(F32) for s in range(NS)] for b in range(NB)]
    peak = None
    for b in range(NB):
        cp_stiff[b].wait()
        total = None
        for s in range(NS):
            size = jnp.abs(stiff_v[b, s] * mask[b][s])
            total = size if total is None else total + size
        sums = dot(ones, split(total), NT)[:8]
        ratio = (sums[:, :BS] + sums[:, BS:]) / diag_v[b:b + 1, :]
        peak = ratio if peak is None else jnp.maximum(peak, ratio)
    mx[0, 0] = jnp.broadcast_to(jnp.max(peak, axis=1, keepdims=True), (8, BS))

    def peak_copy(stage, d):
        dev = (g_peer, z_peer, y_peer)[stage](d)
        row = pl.ds(0, 1)
        return rcopy(mx.at[stage, 0, row], mx.at[stage, d, row], mx_ss.at[stage, d], mx_rs.at[stage, d], dev)

    def send_peak(stage):
        for d in (4, 3, 5, 2, 6, 1, 7):
            peak_copy(stage, d).start()
            pending.append(peak_copy(stage, d).wait_send)

    def take_peak(stage):
        for d in range(1, 8):
            peak_copy(stage, d).wait_recv()
        top = mx[stage, 0, 0:1]
        for d in range(1, 8):
            top = jnp.maximum(top, mx[stage, d, 0:1])
        return top

    send_peak(0)
    for b in range(NB):
        for s in range(NS):
            block = (stiff_v[b, s] * mask[b][s]).T
            high = block.astype(BF16)
            w2[b, s * BS:(s + 1) * BS, 0:BS] = high
            w2[b, s * BS:(s + 1) * BS, BS:2 * BS] = (block - high.astype(F32)).astype(BF16)

    def split_own(k):
        for b in range(NB):
            exts[b] = split(own[k, b])

    split_own(0)

    cp_inv.wait()
    for i in range(NY):
        for c in range(2):
            cols = [(NG * i + 2 * j + c) * BS for j in range(NZL)]
            for j, piece in enumerate(regroup([inv_v[:, col:col + BS] for col in cols], NX, 32)):
                inv_s[NX * c + j, i] = piece

    def inv_copy(d):
        other = mod(g + d, NG)
        return rcopy(inv_s.at[other], inv_r.at[g], inv_ss.at[d], inv_rs.at[d], g_peer(d))

    def send_inv(steps):
        for d in steps:
            inv_copy(d).start()
            pending.append(inv_copy(d).wait_send)

    send_inv((4, 1, 7))
    inv_r[g] = inv_s[g]
    cp_nbr.wait()

    def couple(k):
        wait_halo(k)
        for j in range(4):
            exts[NB + j] = split(ghost[k, j])
        for b in range(NB):
            fields = jnp.concatenate([exts[nbr[b, s]] for s in range(NS)], axis=1)
            coupled = folded(dot(fields, w2[b], NN))
            ksum[k, b] = coupled
            if k < SWEEPS:
                own[k + 1, b] = coupled * rdiag[b]
        if k < SWEEPS:
            fill_halo(k + 1)
            send_halo(k + 1)

    cp_agg.wait()
    row = lax.broadcasted_iota(jnp.int32, (BS, BS), 0)
    turned = 32 * ((row // ROWS) % NX) + ROWS * (row // 64) + row % ROWS
    for b in range(NB):
        which = agg_v[b:b + 1, :]
        cols = slice(b * BS, (b + 1) * BS)
        oh[:, cols] = jnp.where(row == which, 1.0, 0.0).astype(BF16)
        ohs[:, cols] = jnp.where(turned == which, 1.0, 0.0).astype(BF16)

    def dealt(vector):
        pair = dot(jnp.concatenate([split(vector[b]) for b in range(NB)], axis=1), oh[...], NT)
        part = pair[:VEC] + pair[VEC:]
        return regroup([part[8 * i:8 * i + 8] for i in range(3)], NX, 32)

    shares = [dealt(loads_v)]
    couple(0)
    mx[1, 0, 0:1] = take_peak(0)
    send_peak(1)
    send_inv((2, 6))
    split_own(1)
    shares.append(dealt(ksum.at[0]))

    def pass_peak(stage):
        mx[stage, 0, 0:1] = take_peak(stage - 1)
        for d in (4, 3, 5, 2, 6, 1, 7):
            peak_copy(stage, d).start()

    turn = jnp.logical_or(jnp.logical_and(core == 0, zl == 0), jnp.logical_and(core == 1, zl == NZL - 1))
    pl.when(turn)(lambda: pass_peak(2))
    couple(1)
    pl.when(jnp.logical_not(turn))(lambda: pass_peak(2))
    pending.extend(peak_copy(2, d).wait_send for d in range(1, 8))
    send_inv((3, 5))
    split_own(2)
    shares.append(dealt(ksum.at[1]))
    couple(2)
    shares.append(dealt(ksum.at[2]))
    upper = 1.0 + take_peak(2)

    scale = (8.0 / 3.0) / upper
    start = 5.0 / 3.0 - scale
    square = start * start
    final = 4.0 * (5.0 / 3.0) ** 3 - 3.0 * (5.0 / 3.0)
    rho = [start * (4.0 * square - 3.0) * (1.0 / final), (12.0 * square - 3.0) * scale * (1.0 / final),
           start * (scale * scale) * (12.0 / final), scale * (scale * scale) * (4.0 / final)]
    sigma = [rho[1] + (rho[2] + rho[3]), rho[2] + rho[3], rho[3]]

    for j in range(NX):
        i_s[j] = rho[0] * shares[0][j] + rho[1] * shares[1][j] + (rho[2] * shares[2][j] + rho[3] * shares[3][j])
    side = NX * zh + x
    i_r[zl, side] = i_s[x]
    plane = [(dx, dz) for dx in range(NX) for dz in range(NZ) if dx or dz]
    plane.sort(key=lambda p: -hops(p[0], NX) - hops(p[1], NZ))

    def i_copy(dx, dz):
        other = mod(z + dz, NZ)
        ox = mod(x + dx, NX)
        k = NZ * dx + dz
        return rcopy(i_s.at[ox], i_r.at[zl, side], i_ss.at[k], i_rs.at[k],
                     at(y, mod(other, NZL), core, ox, div(other, NZL)))

    def i_arrival(dx, dz):
        came = mod(z + NZ - dz, NZ)
        cx = mod(x + NX - dx, NX)
        k = NZ * dx + dz
        slot = i_r.at[mod(came, NZL), NX * div(came, NZL) + cx]
        return rcopy(slot, slot, i_ss.at[k], i_rs.at[k], z_peer(1))

    for dx, dz in plane:
        i_copy(dx, dz).start()
        pending.append(i_copy(dx, dz).wait_send)

    for b in range(NB):
        res_v[b] = rho[0] * loads_v[b] + rho[1] * ksum[0, b] + rho[2] * ksum[1, b] + rho[3] * ksum[2, b]
        corr_v[b] = sigma[0] * own[0, b] + sigma[1] * own[1, b] + sigma[2] * own[2, b]
    for d in range(1, NG):
        inv_copy(d).wait_recv()
    for i in range(NY):
        block = jnp.concatenate([inv_r[j, i] for j in range(NG)], axis=0).T
        high = block.astype(BF16)
        wc[i, :, 0:BS] = high
        wc[i, :, BS:2 * BS] = (block - high.astype(F32)).astype(BF16)

    for dx, dz in reversed(plane):
        i_arrival(dx, dz).wait_recv()
    tiles = []
    for j in range(NZL):
        total = i_r[j, 0]
        for k in range(1, 2 * NX):
            total = total + i_r[j, k]
        tiles.append(total)
    c_r[y] = jnp.concatenate(regroup(tiles, 3, 32), axis=0)

    def c_copy(d):
        return rcopy(c_r.at[y], c_r.at[y], c_ss.at[d], c_rs.at[d], y_peer(d))

    def c_arrival(d):
        came = mod(y - d + NY, NY)
        return rcopy(c_r.at[came], c_r.at[came], c_ss.at[d], c_rs.at[d], y_peer(d))

    for d in (4, 3, 5, 2, 6, 1, 7):
        c_copy(d).start()
        pending.append(c_copy(d).wait_send)
    full = None
    for pair in ((0, 1), (7, 2), (6, 3), (5, 4)):
        for d in pair:
            if d:
                c_arrival(d).wait_recv()
        for d in pair:
            came = mod(y - d + NY, NY)
            term = dot(split(c_r[came]), wc[came], NN)
            full = term if full is None else full + term
    coarse = folded(full)

    low = lax.broadcasted_iota(jnp.int32, (8, BS), 1) < 64
    t0, t1, t2 = coarse[0:8], coarse[8:16], coarse[16:24]
    u0, u1, u2 = roll(t0, 64), roll(t1, 64), roll(t2, 64)
    d_s[0] = jnp.concatenate([jnp.where(low, t0, u1), jnp.where(low[:4], t2[0:4], u2[4:8])], axis=0)
    d_s[1] = jnp.concatenate([jnp.where(low, u0, t1), jnp.where(low[:4], u2[0:4], t2[4:8])], axis=0)
    d_r[zh, g] = d_s[core]
    around = [(dg, dh) for dg in range(NG) for dh in range(NZH) if dg or dh]
    around.sort(key=lambda p: -4 * p[1] - hops(p[0], NG))

    def d_copy(dg, dh):
        other = mod(g + dg, NG)
        k = NG * dh + dg
        return rcopy(d_s.at[div(other, NX)], d_r.at[zh, g], d_ss.at[k], d_rs.at[k],
                     at(y, zl, div(other, NX), mod(other, NX), mod(zh + dh, NZH)))

    def d_arrival(dg, dh):
        slot = d_r.at[mod(zh + dh, NZH), mod(g + NG - dg, NG)]
        k = NG * dh + dg
        return rcopy(slot, slot, d_ss.at[k], d_rs.at[k], z_peer(1))

    for dg, dh in around:
        d_copy(dg, dh).start()
        pending.append(d_copy(dg, dh).wait_send)
    for wait in pending:
        wait()
    for dg, dh in reversed(around):
        d_arrival(dg, dh).wait_recv()
    sums = []
    for h in range(NZH):
        total = d_r[h, 0]
        for j in range(1, NG):
            total = total + d_r[h, j]
        sums.append(total)

    def tail(value):
        return jnp.concatenate([value[8:12], roll(value[8:12], 64)], axis=0)

    p0, p1 = sums[0][:8], sums[1][:8]
    q0, q1 = tail(sums[0]), tail(sums[1])
    solved = jnp.concatenate([jnp.where(low, p0, roll(p1, 64)), jnp.where(low, roll(p0, 64), p1),
                              jnp.where(low, q0, roll(q1, 64))], axis=0)
    pair = dot(split(solved), ohs[...], NN)
    for b in range(NB):
        cols = slice(b * BS, (b + 1) * BS)
        corr_v[b] = corr_v[b] + (pair[:VEC, cols] + pair[VEC:, cols])


def store(corr_v, res_v, corr_h, res_h, sem):
    one = pltpu.make_async_copy(corr_v, corr_h, sem.at[0])
    two = pltpu.make_async_copy(res_v, res_h, sem.at[1])
    one.start()
    two.start()
    one.wait()
    two.wait()


def shards(loads, diagonal, stiffness, neighbors, slot_mask, send_list, aggregate, coarse_inverse):
    hbm = pl.BlockSpec(memory_space=pltpu.HBM)
    vmem = pl.BlockSpec(memory_space=pltpu.VMEM)
    field = (NB, VEC, BS)
    dma = pltpu.SemaphoreType.DMA
    corr, res = pl.pallas_call(
        kernel,
        out_shape=(pltpu.VMEM(field, F32), pltpu.VMEM(field, F32)),
        in_specs=[hbm] * 8,
        out_specs=(vmem, vmem),
        scratch_shapes=[
            pltpu.SMEM((NB, NS), jnp.int32),
            pltpu.SMEM((NB, NS), jnp.int32),
            pltpu.SMEM((4,), jnp.int32),
            pltpu.VMEM(field, F32),
            pltpu.VMEM((NB, BS), F32),
            pltpu.VMEM((NB, NS, BS, BS), F32),
            pltpu.VMEM((NB, BS), jnp.int32),
            pltpu.VMEM((ROWS, NG * NY * BS), F32),
            pltpu.VMEM((3,) + field, F32),
            pltpu.VMEM((3,) + field, F32),
            pltpu.VMEM((3,) + field, F32),
            pltpu.VMEM((3,) + field, F32),
            pltpu.VMEM((2 * NB, 2 * VEC, BS), BF16),
            pltpu.VMEM((NB, NS * BS, 2 * BS), BF16),
            pltpu.VMEM((3, 8, 8, BS), F32),
            pltpu.VMEM((NG, NY, ROWS, BS), F32),
            pltpu.VMEM((NG, NY, ROWS, BS), F32),
            pltpu.VMEM((NY, BS, 2 * BS), BF16),
            pltpu.VMEM((BS, NB * BS), BF16),
            pltpu.VMEM((BS, NB * BS), BF16),
            pltpu.VMEM((NX, 8, BS), F32),
            pltpu.VMEM((NZL, 2 * NX, 8, BS), F32),
            pltpu.VMEM((NY, VEC, BS), F32),
            pltpu.VMEM((2, 12, BS), F32),
            pltpu.VMEM((NZH, NG, 12, BS), F32),
            dma((11,)),
            dma((3, 2)), dma((3, 2)),
            dma((3, 8)), dma((3, 8)),
            dma((8,)), dma((8,)),
            dma((32,)), dma((32,)),
            dma((8,)), dma((8,)),
            dma((16,)), dma((16,)),
        ],
        compiler_params=pltpu.CompilerParams(collective_id=0, has_side_effects=True, vmem_limit_bytes=58 * 1024 * 1024),
    )(neighbors, slot_mask, send_list, loads, diagonal, stiffness, aggregate, coarse_inverse)
    corr = pltpu.with_memory_space_constraint(corr, pltpu.VMEM)
    res = pltpu.with_memory_space_constraint(res, pltpu.VMEM)
    return pl.pallas_call(
        store,
        out_shape=(jax.ShapeDtypeStruct(field, F32), jax.ShapeDtypeStruct(field, F32)),
        in_specs=[vmem, vmem],
        out_specs=(hbm, hbm),
        scratch_shapes=[dma((2,))],
    )(corr, res)


def solution(mesh):
    both = ("wide", "narrow")
    return jax.shard_map(
        shards,
        mesh=mesh,
        in_specs=(
            P(both, None, None),
            P(both, None),
            P(both, None, None, None),
            P(both, None),
            P(both, None),
            P(both),
            P(both, None),
            P(both, None),
        ),
        out_specs=(P(both, None, None), P(both, None, None)),
        check_vma=False,
    )
```

```python
import jax
import jax.numpy as jnp
from jax import lax
from jax.experimental import pallas as pl
from jax.experimental.pallas import tpu as pltpu
from jax.sharding import PartitionSpec as P

F32 = jnp.float32
BF16 = jnp.bfloat16
MESH = pl.DeviceIdType.MESH
NB, NS, VEC, BS = 4, 4, 24, 128
NX, NY, NZL, NZH = 4, 8, 4, 2
NZ = NZL * NZH
NG = 2 * NX
N_WIDE = NY * NZL * 2
SWEEPS = 2
ROWS = 16
NT = (((1,), (1,)), ((), ()))
NN = (((1,), (0,)), ((), ()))


def split(value):
    high = value.astype(BF16).astype(F32)
    return jnp.concatenate([high, value - high], axis=0).astype(BF16)


def dot(a, b, dims):
    return lax.dot_general(a, b, dims, preferred_element_type=F32)


def folded(full):
    half = full.shape[0] // 2
    cols = full.shape[1] // 2
    return full[:half, :cols] + (full[:half, cols:] + full[half:, :cols])


def roll(value, lanes):
    return value if lanes % BS == 0 else pltpu.roll(value, lanes % BS, 1)


def regroup(tiles, count, width):
    lane = lax.broadcasted_iota(jnp.int32, tiles[0].shape, 1) // width
    out = []
    for i in range(count):
        acc = None
        for j, tile in enumerate(tiles):
            moved = roll(tile, width * (j - i))
            acc = moved if acc is None else jnp.where(lane == j, moved, acc)
        out.append(acc)
    return out


def mod(value, size):
    return lax.rem(value, jnp.int32(size))


def div(value, size):
    return lax.div(value, jnp.int32(size))


def hops(step, size):
    return min(step, size - step)


def kernel(nbr_h, msk_h, snd_h, loads_h, diag_h, stiff_h, agg_h, inv_h, corr_v, res_v,
           nbr, msk, snd, loads_v, diag_v, stiff_v, agg_v, inv_v, own, ksum, sbuf, ghost, exts, w2,
           mx, inv_s, inv_r, wc, oh, ohs, i_s, i_r, c_r, d_s, d_r,
           lsem, halo_ss, halo_rs, mx_ss, mx_rs, inv_ss, inv_rs, i_ss, i_rs, c_ss, c_rs, d_ss, d_rs):
    w = lax.axis_index("wide")
    n = lax.axis_index("narrow")
    core = mod(w, 2)
    zl = mod(div(w, 2), NZL)
    y = div(w, 2 * NZL)
    x = div(n, NZH)
    zh = mod(n, NZH)
    z = zh * NZL + zl
    g = NX * core + x

    cp_loads = pltpu.make_async_copy(loads_h, loads_v, lsem.at[0])
    cp_diag = pltpu.make_async_copy(diag_h, diag_v, lsem.at[1])
    cp_stiff = [pltpu.make_async_copy(stiff_h.at[b], stiff_v.at[b], lsem.at[2 + b]) for b in range(NB)]
    cp_inv = pltpu.make_async_copy(inv_h, inv_v, lsem.at[6])
    cp_agg = pltpu.make_async_copy(agg_h, agg_v, lsem.at[7])
    cp_snd = pltpu.make_async_copy(snd_h, snd, lsem.at[8])
    cp_msk = pltpu.make_async_copy(msk_h, msk, lsem.at[9])
    cp_nbr = pltpu.make_async_copy(nbr_h, nbr, lsem.at[10])
    for cp in [cp_loads, cp_diag] + cp_stiff + [cp_snd]:
        cp.start()

    def at(y_, zl_, core_, x_, zh_):
        return ((y_ * NZL + zl_) * 2 + core_, x_ * NZH + zh_)

    def g_peer(d):
        other = mod(g + d, NG)
        return at(y, zl, div(other, NX), mod(other, NX), zh)

    def z_peer(d):
        other = mod(z + d, NZ)
        return at(y, mod(other, NZL), core, x, div(other, NZL))

    def y_peer(d):
        return at(mod(y + d, NY), zl, core, x, zh)

    pending = []

    def rcopy(src, dst, ss, rs, dev):
        return pltpu.make_async_remote_copy(src_ref=src, dst_ref=dst, send_sem=ss, recv_sem=rs,
                                            device_id=dev, device_id_type=MESH)

    barrier = pltpu.get_barrier_semaphore()

    def greet(dev):
        pl.semaphore_signal(barrier, inc=1, device_id=dev, device_id_type=MESH)

    left_far = jnp.logical_and(core == 0, w > 0)
    right_far = jnp.logical_and(core == 1, w < N_WIDE - 1)
    pl.when(left_far)(lambda: greet((w - 1, n)))
    pl.when(right_far)(lambda: greet((w + 1, n)))
    for d in (4, 3, 5, 2, 6, 1, 7):
        greet(y_peer(d))
        greet(z_peer(d))
    for d in (2, 6, 1, 3, 5, 7, 4):
        greet(g_peer(d))

    for cp in (cp_msk, cp_nbr, cp_inv, cp_agg):
        cp.start()

    @pl.when(w == 0)
    def _():
        ghost[:, 0:2] = jnp.zeros((3, 2, VEC, BS), F32)

    @pl.when(w == N_WIDE - 1)
    def _():
        ghost[:, 2:4] = jnp.zeros((3, 2, VEC, BS), F32)

    cp_loads.wait()
    cp_diag.wait()
    rdiag = [1.0 / diag_v[b:b + 1, :] for b in range(NB)]
    for b in range(NB):
        own[0, b] = loads_v[b] * rdiag[b]
    cp_snd.wait()

    def to_left(k):
        return rcopy(sbuf.at[k, pl.ds(0, 2)], ghost.at[k, pl.ds(2, 2)], halo_ss.at[k, 0], halo_rs.at[k, 0], (w - 1, n))

    def to_right(k):
        return rcopy(sbuf.at[k, pl.ds(2, 2)], ghost.at[k, pl.ds(0, 2)], halo_ss.at[k, 1], halo_rs.at[k, 1], (w + 1, n))

    def fill_halo(k):
        for j in range(4):
            sbuf[k, j] = own[k, snd[j]]

    def send_halo(k):
        pl.when(w > 0)(lambda: to_left(k).start())
        pl.when(w < N_WIDE - 1)(lambda: to_right(k).start())
        pending.append(lambda: pl.when(w > 0)(lambda: to_left(k).wait_send()))
        pending.append(lambda: pl.when(w < N_WIDE - 1)(lambda: to_right(k).wait_send()))

    def wait_halo(k):
        pl.when(w < N_WIDE - 1)(lambda: to_left(k).wait_recv())
        pl.when(w > 0)(lambda: to_right(k).wait_recv())

    fill_halo(0)

    @pl.when(jnp.logical_or(left_far, right_far))
    def _():
        pl.semaphore_wait(barrier, 22)

    @pl.when(jnp.logical_not(jnp.logical_or(left_far, right_far)))
    def _():
        pl.semaphore_wait(barrier, 21)

    send_halo(0)

    cp_msk.wait()
    ones = jnp.ones((16, BS), BF16)
    mask = [[msk[b, s].astype(F32) for s in range(NS)] for b in range(NB)]
    peak = None
    for b in range(NB):
        cp_stiff[b].wait()
        total = None
        for s in range(NS):
            size = jnp.abs(stiff_v[b, s] * mask[b][s])
            total = size if total is None else total + size
        sums = dot(ones, split(total), NT)[:8]
        ratio = (sums[:, :BS] + sums[:, BS:]) / diag_v[b:b + 1, :]
        peak = ratio if peak is None else jnp.maximum(peak, ratio)
    mx[0, 0] = jnp.broadcast_to(jnp.max(peak, axis=1, keepdims=True), (8, BS))

    def peak_copy(stage, d):
        dev = (g_peer, z_peer, y_peer)[stage](d)
        row = pl.ds(0, 1)
        return rcopy(mx.at[stage, 0, row], mx.at[stage, d, row], mx_ss.at[stage, d], mx_rs.at[stage, d], dev)

    def send_peak(stage):
        for d in (4, 3, 5, 2, 6, 1, 7):
            peak_copy(stage, d).start()
            pending.append(peak_copy(stage, d).wait_send)

    def take_peak(stage):
        for d in range(1, 8):
            peak_copy(stage, d).wait_recv()
        top = mx[stage, 0, 0:1]
        for d in range(1, 8):
            top = jnp.maximum(top, mx[stage, d, 0:1])
        return top

    send_peak(0)
    for b in range(NB):
        for s in range(NS):
            block = (stiff_v[b, s] * mask[b][s]).T
            high = block.astype(BF16)
            w2[b, s * BS:(s + 1) * BS, 0:BS] = high
            w2[b, s * BS:(s + 1) * BS, BS:2 * BS] = (block - high.astype(F32)).astype(BF16)

    def split_own(k):
        for b in range(NB):
            exts[b] = split(own[k, b])

    split_own(0)

    cp_inv.wait()
    for i in range(NY):
        for c in range(2):
            cols = [(NG * i + 2 * j + c) * BS for j in range(NZL)]
            for j, piece in enumerate(regroup([inv_v[:, col:col + BS] for col in cols], NX, 32)):
                inv_s[NX * c + j, i] = piece

    def inv_copy(d):
        other = mod(g + d, NG)
        return rcopy(inv_s.at[other], inv_r.at[g], inv_ss.at[d], inv_rs.at[d], g_peer(d))

    def send_inv(steps):
        for d in steps:
            inv_copy(d).start()
            pending.append(inv_copy(d).wait_send)

    send_inv((4, 1, 7))
    inv_r[g] = inv_s[g]
    cp_nbr.wait()

    def couple(k):
        wait_halo(k)
        for j in range(4):
            exts[NB + j] = split(ghost[k, j])
        for b in range(NB):
            fields = jnp.concatenate([exts[nbr[b, s]] for s in range(NS)], axis=1)
            coupled = folded(dot(fields, w2[b], NN))
            ksum[k, b] = coupled
            if k < SWEEPS:
                own[k + 1, b] = coupled * rdiag[b]
        if k < SWEEPS:
            fill_halo(k + 1)
            send_halo(k + 1)

    cp_agg.wait()
    row = lax.broadcasted_iota(jnp.int32, (BS, BS), 0)
    turned = 32 * ((row // ROWS) % NX) + ROWS * (row // 64) + row % ROWS
    for b in range(NB):
        which = agg_v[b:b + 1, :]
        cols = slice(b * BS, (b + 1) * BS)
        oh[:, cols] = jnp.where(row == which, 1.0, 0.0).astype(BF16)
        ohs[:, cols] = jnp.where(turned == which, 1.0, 0.0).astype(BF16)

    def dealt(vector):
        pair = dot(jnp.concatenate([split(vector[b]) for b in range(NB)], axis=1), oh[...], NT)
        part = pair[:VEC] + pair[VEC:]
        return regroup([part[8 * i:8 * i + 8] for i in range(3)], NX, 32)

    shares = [dealt(loads_v)]
    couple(0)
    mx[1, 0, 0:1] = take_peak(0)
    send_peak(1)
    send_inv((2, 6))
    split_own(1)
    shares.append(dealt(ksum.at[0]))

    def pass_peak(stage):
        mx[stage, 0, 0:1] = take_peak(stage - 1)
        for d in (4, 3, 5, 2, 6, 1, 7):
            peak_copy(stage, d).start()

    turn = jnp.logical_or(jnp.logical_and(core == 0, zl == 0), jnp.logical_and(core == 1, zl == NZL - 1))
    pl.when(turn)(lambda: pass_peak(2))
    couple(1)
    pl.when(jnp.logical_not(turn))(lambda: pass_peak(2))
    pending.extend(peak_copy(2, d).wait_send for d in range(1, 8))
    send_inv((3, 5))
    split_own(2)
    shares.append(dealt(ksum.at[1]))
    couple(2)
    shares.append(dealt(ksum.at[2]))
    upper = 1.0 + take_peak(2)

    scale = (8.0 / 3.0) / upper
    start = 5.0 / 3.0 - scale
    square = start * start
    final = 4.0 * (5.0 / 3.0) ** 3 - 3.0 * (5.0 / 3.0)
    rho = [start * (4.0 * square - 3.0) * (1.0 / final), (12.0 * square - 3.0) * scale * (1.0 / final),
           start * (scale * scale) * (12.0 / final), scale * (scale * scale) * (4.0 / final)]
    sigma = [rho[1] + (rho[2] + rho[3]), rho[2] + rho[3], rho[3]]

    for j in range(NX):
        i_s[j] = rho[0] * shares[0][j] + rho[1] * shares[1][j] + (rho[2] * shares[2][j] + rho[3] * shares[3][j])
    side = NX * zh + x
    i_r[zl, side] = i_s[x]
    plane = [(dx, dz) for dx in range(NX) for dz in range(NZ) if dx or dz]
    plane.sort(key=lambda p: (-hops(p[1], NZ), -hops(p[0], NX)))

    def i_copy(dx, dz):
        other = mod(z + dz, NZ)
        ox = mod(x + dx, NX)
        k = NZ * dx + dz
        return rcopy(i_s.at[ox], i_r.at[zl, side], i_ss.at[k], i_rs.at[k],
                     at(y, mod(other, NZL), core, ox, div(other, NZL)))

    def i_arrival(dx, dz):
        came = mod(z + NZ - dz, NZ)
        cx = mod(x + NX - dx, NX)
        k = NZ * dx + dz
        slot = i_r.at[mod(came, NZL), NX * div(came, NZL) + cx]
        return rcopy(slot, slot, i_ss.at[k], i_rs.at[k], z_peer(1))

    for dx, dz in plane:
        i_copy(dx, dz).start()
        pending.append(i_copy(dx, dz).wait_send)

    for b in range(NB):
        res_v[b] = rho[0] * loads_v[b] + rho[1] * ksum[0, b] + rho[2] * ksum[1, b] + rho[3] * ksum[2, b]
        corr_v[b] = sigma[0] * own[0, b] + sigma[1] * own[1, b] + sigma[2] * own[2, b]
    for d in range(1, NG):
        inv_copy(d).wait_recv()
    for i in range(NY):
        block = jnp.concatenate([inv_r[j, i] for j in range(NG)], axis=0).T
        high = block.astype(BF16)
        wc[i, :, 0:BS] = high
        wc[i, :, BS:2 * BS] = (block - high.astype(F32)).astype(BF16)

    for dx, dz in reversed(plane):
        i_arrival(dx, dz).wait_recv()
    tiles = []
    for j in range(NZL):
        total = i_r[j, 0]
        for k in range(1, 2 * NX):
            total = total + i_r[j, k]
        tiles.append(total)
    c_r[y] = jnp.concatenate(regroup(tiles, 3, 32), axis=0)

    def c_copy(d):
        return rcopy(c_r.at[y], c_r.at[y], c_ss.at[d], c_rs.at[d], y_peer(d))

    def c_arrival(d):
        came = mod(y - d + NY, NY)
        return rcopy(c_r.at[came], c_r.at[came], c_ss.at[d], c_rs.at[d], y_peer(d))

    for d in (4, 3, 5, 2, 6, 1, 7):
        c_copy(d).start()
        pending.append(c_copy(d).wait_send)
    full = None
    for pair in ((0, 1), (7, 2), (6, 3), (5, 4)):
        for d in pair:
            if d:
                c_arrival(d).wait_recv()
        for d in pair:
            came = mod(y - d + NY, NY)
            term = dot(split(c_r[came]), wc[came], NN)
            full = term if full is None else full + term
    coarse = folded(full)

    low = lax.broadcasted_iota(jnp.int32, (8, BS), 1) < 64
    t0, t1, t2 = coarse[0:8], coarse[8:16], coarse[16:24]
    u0, u1, u2 = roll(t0, 64), roll(t1, 64), roll(t2, 64)
    d_s[0] = jnp.concatenate([jnp.where(low, t0, u1), jnp.where(low[:4], t2[0:4], u2[4:8])], axis=0)
    d_s[1] = jnp.concatenate([jnp.where(low, u0, t1), jnp.where(low[:4], u2[0:4], t2[4:8])], axis=0)
    d_r[zh, g] = d_s[core]
    around = [(dg, dh) for dg in range(NG) for dh in range(NZH) if dg or dh]
    around.sort(key=lambda p: -4 * p[1] - hops(p[0] % NX, NX))

    def d_copy(dg, dh):
        other = mod(g + dg, NG)
        k = NG * dh + dg
        return rcopy(d_s.at[div(other, NX)], d_r.at[zh, g], d_ss.at[k], d_rs.at[k],
                     at(y, zl, div(other, NX), mod(other, NX), mod(zh + dh, NZH)))

    def d_arrival(dg, dh):
        slot = d_r.at[mod(zh + dh, NZH), mod(g + NG - dg, NG)]
        k = NG * dh + dg
        return rcopy(slot, slot, d_ss.at[k], d_rs.at[k], z_peer(1))

    for dg, dh in around:
        d_copy(dg, dh).start()
        pending.append(d_copy(dg, dh).wait_send)
    for wait in pending:
        wait()
    for dg, dh in reversed(around):
        d_arrival(dg, dh).wait_recv()
    sums = []
    for h in range(NZH):
        total = d_r[h, 0]
        for j in range(1, NG):
            total = total + d_r[h, j]
        sums.append(total)

    def tail(value):
        return jnp.concatenate([value[8:12], roll(value[8:12], 64)], axis=0)

    p0, p1 = sums[0][:8], sums[1][:8]
    q0, q1 = tail(sums[0]), tail(sums[1])
    solved = jnp.concatenate([jnp.where(low, p0, roll(p1, 64)), jnp.where(low, roll(p0, 64), p1),
                              jnp.where(low, q0, roll(q1, 64))], axis=0)
    pair = dot(split(solved), ohs[...], NN)
    for b in range(NB):
        cols = slice(b * BS, (b + 1) * BS)
        corr_v[b] = corr_v[b] + (pair[:VEC, cols] + pair[VEC:, cols])


def store(corr_v, res_v, corr_h, res_h, sem):
    one = pltpu.make_async_copy(corr_v, corr_h, sem.at[0])
    two = pltpu.make_async_copy(res_v, res_h, sem.at[1])
    one.start()
    two.start()
    one.wait()
    two.wait()


def shards(loads, diagonal, stiffness, neighbors, slot_mask, send_list, aggregate, coarse_inverse):
    hbm = pl.BlockSpec(memory_space=pltpu.HBM)
    vmem = pl.BlockSpec(memory_space=pltpu.VMEM)
    field = (NB, VEC, BS)
    dma = pltpu.SemaphoreType.DMA
    corr, res = pl.pallas_call(
        kernel,
        out_shape=(pltpu.VMEM(field, F32), pltpu.VMEM(field, F32)),
        in_specs=[hbm] * 8,
        out_specs=(vmem, vmem),
        scratch_shapes=[
            pltpu.SMEM((NB, NS), jnp.int32),
            pltpu.SMEM((NB, NS), jnp.int32),
            pltpu.SMEM((4,), jnp.int32),
            pltpu.VMEM(field, F32),
            pltpu.VMEM((NB, BS), F32),
            pltpu.VMEM((NB, NS, BS, BS), F32),
            pltpu.VMEM((NB, BS), jnp.int32),
            pltpu.VMEM((ROWS, NG * NY * BS), F32),
            pltpu.VMEM((3,) + field, F32),
            pltpu.VMEM((3,) + field, F32),
            pltpu.VMEM((3,) + field, F32),
            pltpu.VMEM((3,) + field, F32),
            pltpu.VMEM((2 * NB, 2 * VEC, BS), BF16),
            pltpu.VMEM((NB, NS * BS, 2 * BS), BF16),
            pltpu.VMEM((3, 8, 8, BS), F32),
            pltpu.VMEM((NG, NY, ROWS, BS), F32),
            pltpu.VMEM((NG, NY, ROWS, BS), F32),
            pltpu.VMEM((NY, BS, 2 * BS), BF16),
            pltpu.VMEM((BS, NB * BS), BF16),
            pltpu.VMEM((BS, NB * BS), BF16),
            pltpu.VMEM((NX, 8, BS), F32),
            pltpu.VMEM((NZL, 2 * NX, 8, BS), F32),
            pltpu.VMEM((NY, VEC, BS), F32),
            pltpu.VMEM((2, 12, BS), F32),
            pltpu.VMEM((NZH, NG, 12, BS), F32),
            dma((11,)),
            dma((3, 2)), dma((3, 2)),
            dma((3, 8)), dma((3, 8)),
            dma((8,)), dma((8,)),
            dma((32,)), dma((32,)),
            dma((8,)), dma((8,)),
            dma((16,)), dma((16,)),
        ],
        compiler_params=pltpu.CompilerParams(collective_id=0, has_side_effects=True, vmem_limit_bytes=58 * 1024 * 1024),
    )(neighbors, slot_mask, send_list, loads, diagonal, stiffness, aggregate, coarse_inverse)
    corr = pltpu.with_memory_space_constraint(corr, pltpu.VMEM)
    res = pltpu.with_memory_space_constraint(res, pltpu.VMEM)
    return pl.pallas_call(
        store,
        out_shape=(jax.ShapeDtypeStruct(field, F32), jax.ShapeDtypeStruct(field, F32)),
        in_specs=[vmem, vmem],
        out_specs=(hbm, hbm),
        scratch_shapes=[dma((2,))],
    )(corr, res)


def solution(mesh):
    both = ("wide", "narrow")
    return jax.shard_map(
        shards,
        mesh=mesh,
        in_specs=(
            P(both, None, None),
            P(both, None),
            P(both, None, None, None),
            P(both, None),
            P(both, None),
            P(both),
            P(both, None),
            P(both, None),
        ),
        out_specs=(P(both, None, None), P(both, None, None)),
        check_vma=False,
    )
```

```python
import jax
import jax.numpy as jnp
from jax import lax
from jax.experimental import pallas as pl
from jax.experimental.pallas import tpu as pltpu
from jax.sharding import PartitionSpec as P

F32 = jnp.float32
BF16 = jnp.bfloat16
MESH = pl.DeviceIdType.MESH
NB, NS, VEC, BS = 4, 4, 24, 128
NX, NY, NZL, NZH = 4, 8, 4, 2
NZ = NZL * NZH
NG = 2 * NX
N_WIDE = NY * NZL * 2
SWEEPS = 2
ROWS = 16
NT = (((1,), (1,)), ((), ()))
NN = (((1,), (0,)), ((), ()))


def split(value):
    high = value.astype(BF16).astype(F32)
    return jnp.concatenate([high, value - high], axis=0).astype(BF16)


def dot(a, b, dims):
    return lax.dot_general(a, b, dims, preferred_element_type=F32)


def folded(full):
    half = full.shape[0] // 2
    cols = full.shape[1] // 2
    return full[:half, :cols] + (full[:half, cols:] + full[half:, :cols])


def roll(value, lanes):
    return value if lanes % BS == 0 else pltpu.roll(value, lanes % BS, 1)


def regroup(tiles, count, width):
    lane = lax.broadcasted_iota(jnp.int32, tiles[0].shape, 1) // width
    out = []
    for i in range(count):
        acc = None
        for j, tile in enumerate(tiles):
            moved = roll(tile, width * (j - i))
            acc = moved if acc is None else jnp.where(lane == j, moved, acc)
        out.append(acc)
    return out


def mod(value, size):
    return lax.rem(value, jnp.int32(size))


def div(value, size):
    return lax.div(value, jnp.int32(size))


def hops(step, size):
    return min(step, size - step)


def kernel(nbr_h, msk_h, snd_h, loads_h, diag_h, stiff_h, agg_h, inv_h, corr_v, res_v,
           nbr, msk, snd, loads_v, diag_v, stiff_v, agg_v, inv_v, own, ksum, sbuf, ghost, exts, w2,
           mx, inv_s, inv_r, wc, oh, ohs, i_s, i_r, c_r, d_s, d_r,
           lsem, halo_ss, halo_rs, mx_ss, mx_rs, inv_ss, inv_rs, i_ss, i_rs, c_ss, c_rs, d_ss, d_rs):
    w = lax.axis_index("wide")
    n = lax.axis_index("narrow")
    core = mod(w, 2)
    zl = mod(div(w, 2), NZL)
    y = div(w, 2 * NZL)
    x = div(n, NZH)
    zh = mod(n, NZH)
    z = zh * NZL + zl
    g = NX * core + x

    cp_loads = pltpu.make_async_copy(loads_h, loads_v, lsem.at[0])
    cp_diag = pltpu.make_async_copy(diag_h, diag_v, lsem.at[1])
    cp_stiff = [pltpu.make_async_copy(stiff_h.at[b], stiff_v.at[b], lsem.at[2 + b]) for b in range(NB)]
    cp_inv = pltpu.make_async_copy(inv_h, inv_v, lsem.at[6])
    cp_agg = pltpu.make_async_copy(agg_h, agg_v, lsem.at[7])
    cp_snd = pltpu.make_async_copy(snd_h, snd, lsem.at[8])
    cp_msk = pltpu.make_async_copy(msk_h, msk, lsem.at[9])
    cp_nbr = pltpu.make_async_copy(nbr_h, nbr, lsem.at[10])
    for cp in [cp_loads, cp_diag, cp_snd, cp_msk, cp_nbr] + cp_stiff + [cp_inv, cp_agg]:
        cp.start()

    def at(y_, zl_, core_, x_, zh_):
        return ((y_ * NZL + zl_) * 2 + core_, x_ * NZH + zh_)

    def g_peer(d):
        other = mod(g + d, NG)
        return at(y, zl, div(other, NX), mod(other, NX), zh)

    def z_peer(d):
        other = mod(z + d, NZ)
        return at(y, mod(other, NZL), core, x, div(other, NZL))

    def y_peer(d):
        return at(mod(y + d, NY), zl, core, x, zh)

    pending = []

    def rcopy(src, dst, ss, rs, dev):
        return pltpu.make_async_remote_copy(src_ref=src, dst_ref=dst, send_sem=ss, recv_sem=rs,
                                            device_id=dev, device_id_type=MESH)

    barrier = pltpu.get_barrier_semaphore()

    def greet(dev):
        pl.semaphore_signal(barrier, inc=1, device_id=dev, device_id_type=MESH)

    left_far = jnp.logical_and(core == 0, w > 0)
    right_far = jnp.logical_and(core == 1, w < N_WIDE - 1)
    pl.when(left_far)(lambda: greet((w - 1, n)))
    pl.when(right_far)(lambda: greet((w + 1, n)))
    for d in range(1, 8):
        greet(g_peer(d))
        greet(z_peer(d))
        greet(y_peer(d))

    @pl.when(w == 0)
    def _():
        ghost[:, 0:2] = jnp.zeros((3, 2, VEC, BS), F32)

    @pl.when(w == N_WIDE - 1)
    def _():
        ghost[:, 2:4] = jnp.zeros((3, 2, VEC, BS), F32)

    cp_loads.wait()
    cp_diag.wait()
    rdiag = [1.0 / diag_v[b:b + 1, :] for b in range(NB)]
    for b in range(NB):
        own[0, b] = loads_v[b] * rdiag[b]
    cp_snd.wait()

    def to_left(k):
        return rcopy(sbuf.at[k, pl.ds(0, 2)], ghost.at[k, pl.ds(2, 2)], halo_ss.at[k, 0], halo_rs.at[k, 0], (w - 1, n))

    def to_right(k):
        return rcopy(sbuf.at[k, pl.ds(2, 2)], ghost.at[k, pl.ds(0, 2)], halo_ss.at[k, 1], halo_rs.at[k, 1], (w + 1, n))

    def fill_halo(k):
        for j in range(4):
            sbuf[k, j] = own[k, snd[j]]

    def send_halo(k):
        pl.when(w > 0)(lambda: to_left(k).start())
        pl.when(w < N_WIDE - 1)(lambda: to_right(k).start())
        pending.append(lambda: pl.when(w > 0)(lambda: to_left(k).wait_send()))
        pending.append(lambda: pl.when(w < N_WIDE - 1)(lambda: to_right(k).wait_send()))

    def split_ghosts(k, first):
        for j in range(2):
            exts[NB + first + j] = split(ghost[k, first + j])

    def wait_halo(k):
        pl.when(core == 0)(lambda: to_left(k).wait_recv())
        pl.when(core == 1)(lambda: to_right(k).wait_recv())
        split_ghosts(k, 2 - 2 * core)
        pl.when(right_far)(lambda: to_left(k).wait_recv())
        pl.when(left_far)(lambda: to_right(k).wait_recv())
        split_ghosts(k, 2 * core)

    fill_halo(0)

    @pl.when(jnp.logical_or(left_far, right_far))
    def _():
        pl.semaphore_wait(barrier, 22)

    @pl.when(jnp.logical_not(jnp.logical_or(left_far, right_far)))
    def _():
        pl.semaphore_wait(barrier, 21)

    send_halo(0)

    cp_msk.wait()
    ones = jnp.ones((16, BS), BF16)
    mask = [[msk[b, s].astype(F32) for s in range(NS)] for b in range(NB)]
    peak = None
    for b in range(NB):
        cp_stiff[b].wait()
        total = None
        for s in range(NS):
            size = jnp.abs(stiff_v[b, s] * mask[b][s])
            total = size if total is None else total + size
        sums = dot(ones, split(total), NT)[:8]
        ratio = (sums[:, :BS] + sums[:, BS:]) / diag_v[b:b + 1, :]
        peak = ratio if peak is None else jnp.maximum(peak, ratio)
    mx[0, 0] = jnp.broadcast_to(jnp.max(peak, axis=1, keepdims=True), (8, BS))

    def peak_copy(stage, d):
        dev = (g_peer, z_peer, y_peer)[stage](d)
        row = pl.ds(0, 1)
        return rcopy(mx.at[stage, 0, row], mx.at[stage, d, row], mx_ss.at[stage, d], mx_rs.at[stage, d], dev)

    def send_peak(stage):
        for d in (4, 3, 5, 2, 6, 1, 7):
            peak_copy(stage, d).start()
            pending.append(peak_copy(stage, d).wait_send)

    def take_peak(stage):
        for d in range(1, 8):
            peak_copy(stage, d).wait_recv()
        top = mx[stage, 0, 0:1]
        for d in range(1, 8):
            top = jnp.maximum(top, mx[stage, d, 0:1])
        return top

    send_peak(0)
    for b in range(NB):
        for s in range(NS):
            block = (stiff_v[b, s] * mask[b][s]).T
            high = block.astype(BF16)
            w2[b, s * BS:(s + 1) * BS, 0:BS] = high
            w2[b, s * BS:(s + 1) * BS, BS:2 * BS] = (block - high.astype(F32)).astype(BF16)

    def split_own(k):
        for b in range(NB):
            exts[b] = split(own[k, b])

    split_own(0)

    cp_inv.wait()
    for i in range(NY):
        for c in range(2):
            cols = [(NG * i + 2 * j + c) * BS for j in range(NZL)]
            for j, piece in enumerate(regroup([inv_v[:, col:col + BS] for col in cols], NX, 32)):
                inv_s[NX * c + j, i] = piece

    def inv_copy(d):
        other = mod(g + d, NG)
        return rcopy(inv_s.at[other], inv_r.at[g], inv_ss.at[d], inv_rs.at[d], g_peer(d))

    def send_inv(steps):
        for d in steps:
            inv_copy(d).start()
            pending.append(inv_copy(d).wait_send)

    send_inv((4, 1, 7))
    inv_r[g] = inv_s[g]
    cp_nbr.wait()

    def couple(k):
        wait_halo(k)
        for b in range(NB):
            fields = jnp.concatenate([exts[nbr[b, s]] for s in range(NS)], axis=1)
            coupled = folded(dot(fields, w2[b], NN))
            ksum[k, b] = coupled
            if k < SWEEPS:
                own[k + 1, b] = coupled * rdiag[b]
        if k < SWEEPS:
            fill_halo(k + 1)
            send_halo(k + 1)

    cp_agg.wait()
    row = lax.broadcasted_iota(jnp.int32, (BS, BS), 0)
    turned = 32 * ((row // ROWS) % NX) + ROWS * (row // 64) + row % ROWS
    for b in range(NB):
        which = agg_v[b:b + 1, :]
        cols = slice(b * BS, (b + 1) * BS)
        oh[:, cols] = jnp.where(row == which, 1.0, 0.0).astype(BF16)
        ohs[:, cols] = jnp.where(turned == which, 1.0, 0.0).astype(BF16)

    def dealt(vector):
        pair = dot(jnp.concatenate([split(vector[b]) for b in range(NB)], axis=1), oh[...], NT)
        part = pair[:VEC] + pair[VEC:]
        return regroup([part[8 * i:8 * i + 8] for i in range(3)], NX, 32)

    shares = [dealt(loads_v)]
    couple(0)
    mx[1, 0, 0:1] = take_peak(0)
    send_peak(1)
    send_inv((2, 6))
    split_own(1)
    shares.append(dealt(ksum.at[0]))

    def pass_peak(stage):
        mx[stage, 0, 0:1] = take_peak(stage - 1)
        for d in (4, 3, 5, 2, 6, 1, 7):
            peak_copy(stage, d).start()

    turn = jnp.logical_or(jnp.logical_and(core == 0, zl == 0), jnp.logical_and(core == 1, zl == NZL - 1))
    pl.when(turn)(lambda: pass_peak(2))
    couple(1)
    pl.when(jnp.logical_not(turn))(lambda: pass_peak(2))
    pending.extend(peak_copy(2, d).wait_send for d in range(1, 8))
    send_inv((3, 5))
    split_own(2)
    shares.append(dealt(ksum.at[1]))
    couple(2)
    shares.append(dealt(ksum.at[2]))
    upper = 1.0 + take_peak(2)

    scale = (8.0 / 3.0) / upper
    start = 5.0 / 3.0 - scale
    square = start * start
    final = 4.0 * (5.0 / 3.0) ** 3 - 3.0 * (5.0 / 3.0)
    rho = [start * (4.0 * square - 3.0) * (1.0 / final), (12.0 * square - 3.0) * scale * (1.0 / final),
           start * (scale * scale) * (12.0 / final), scale * (scale * scale) * (4.0 / final)]
    sigma = [rho[1] + (rho[2] + rho[3]), rho[2] + rho[3], rho[3]]

    for j in range(NX):
        i_s[j] = rho[0] * shares[0][j] + rho[1] * shares[1][j] + (rho[2] * shares[2][j] + rho[3] * shares[3][j])
    side = NX * zh + x
    i_r[zl, side] = i_s[x]
    plane = [(dx, dz) for dx in range(NX) for dz in range(NZ) if dx or dz]
    plane.sort(key=lambda p: -hops(p[0], NX) - hops(p[1], NZ))

    def i_copy(dx, dz):
        other = mod(z + dz, NZ)
        ox = mod(x + dx, NX)
        k = NZ * dx + dz
        return rcopy(i_s.at[ox], i_r.at[zl, side], i_ss.at[k], i_rs.at[k],
                     at(y, mod(other, NZL), core, ox, div(other, NZL)))

    def i_arrival(dx, dz):
        came = mod(z + NZ - dz, NZ)
        cx = mod(x + NX - dx, NX)
        k = NZ * dx + dz
        slot = i_r.at[mod(came, NZL), NX * div(came, NZL) + cx]
        return rcopy(slot, slot, i_ss.at[k], i_rs.at[k], z_peer(1))

    for dx, dz in plane:
        i_copy(dx, dz).start()
        pending.append(i_copy(dx, dz).wait_send)

    for b in range(NB):
        res_v[b] = rho[0] * loads_v[b] + rho[1] * ksum[0, b] + rho[2] * ksum[1, b] + rho[3] * ksum[2, b]
        corr_v[b] = sigma[0] * own[0, b] + sigma[1] * own[1, b] + sigma[2] * own[2, b]
    for d in range(1, NG):
        inv_copy(d).wait_recv()
    for i in range(NY):
        block = jnp.concatenate([inv_r[j, i] for j in range(NG)], axis=0).T
        high = block.astype(BF16)
        wc[i, :, 0:BS] = high
        wc[i, :, BS:2 * BS] = (block - high.astype(F32)).astype(BF16)

    for dx, dz in reversed(plane):
        i_arrival(dx, dz).wait_recv()
    tiles = []
    for j in range(NZL):
        total = i_r[j, 0]
        for k in range(1, 2 * NX):
            total = total + i_r[j, k]
        tiles.append(total)
    c_r[y] = jnp.concatenate(regroup(tiles, 3, 32), axis=0)

    def c_copy(d):
        return rcopy(c_r.at[y], c_r.at[y], c_ss.at[d], c_rs.at[d], y_peer(d))

    def c_arrival(d):
        came = mod(y - d + NY, NY)
        return rcopy(c_r.at[came], c_r.at[came], c_ss.at[d], c_rs.at[d], y_peer(d))

    for d in (4, 3, 5, 2, 6, 1, 7):
        c_copy(d).start()
        pending.append(c_copy(d).wait_send)
    full = None
    for pair in ((0, 1), (7, 2), (6, 3), (5, 4)):
        for d in pair:
            if d:
                c_arrival(d).wait_recv()
        for d in pair:
            came = mod(y - d + NY, NY)
            term = dot(split(c_r[came]), wc[came], NN)
            full = term if full is None else full + term
    coarse = folded(full)

    low = lax.broadcasted_iota(jnp.int32, (8, BS), 1) < 64
    t0, t1, t2 = coarse[0:8], coarse[8:16], coarse[16:24]
    u0, u1, u2 = roll(t0, 64), roll(t1, 64), roll(t2, 64)
    d_s[0] = jnp.concatenate([jnp.where(low, t0, u1), jnp.where(low[:4], t2[0:4], u2[4:8])], axis=0)
    d_s[1] = jnp.concatenate([jnp.where(low, u0, t1), jnp.where(low[:4], u2[0:4], t2[4:8])], axis=0)
    d_r[zh, g] = d_s[core]
    around = [(dg, dh) for dg in range(NG) for dh in range(NZH) if dg or dh]
    around.sort(key=lambda p: -4 * p[1] - hops(p[0], NG))

    def d_copy(dg, dh):
        other = mod(g + dg, NG)
        k = NG * dh + dg
        return rcopy(d_s.at[div(other, NX)], d_r.at[zh, g], d_ss.at[k], d_rs.at[k],
                     at(y, zl, div(other, NX), mod(other, NX), mod(zh + dh, NZH)))

    def d_arrival(dg, dh):
        slot = d_r.at[mod(zh + dh, NZH), mod(g + NG - dg, NG)]
        k = NG * dh + dg
        return rcopy(slot, slot, d_ss.at[k], d_rs.at[k], z_peer(1))

    for dg, dh in around:
        d_copy(dg, dh).start()
        pending.append(d_copy(dg, dh).wait_send)
    for wait in pending:
        wait()
    for dg, dh in reversed(around):
        d_arrival(dg, dh).wait_recv()
    sums = []
    for h in range(NZH):
        total = d_r[h, 0]
        for j in range(1, NG):
            total = total + d_r[h, j]
        sums.append(total)

    def tail(value):
        return jnp.concatenate([value[8:12], roll(value[8:12], 64)], axis=0)

    p0, p1 = sums[0][:8], sums[1][:8]
    q0, q1 = tail(sums[0]), tail(sums[1])
    solved = jnp.concatenate([jnp.where(low, p0, roll(p1, 64)), jnp.where(low, roll(p0, 64), p1),
                              jnp.where(low, q0, roll(q1, 64))], axis=0)
    pair = dot(split(solved), ohs[...], NN)
    for b in range(NB):
        cols = slice(b * BS, (b + 1) * BS)
        corr_v[b] = corr_v[b] + (pair[:VEC, cols] + pair[VEC:, cols])


def store(corr_v, res_v, corr_h, res_h, sem):
    one = pltpu.make_async_copy(corr_v, corr_h, sem.at[0])
    two = pltpu.make_async_copy(res_v, res_h, sem.at[1])
    one.start()
    two.start()
    one.wait()
    two.wait()


def shards(loads, diagonal, stiffness, neighbors, slot_mask, send_list, aggregate, coarse_inverse):
    hbm = pl.BlockSpec(memory_space=pltpu.HBM)
    vmem = pl.BlockSpec(memory_space=pltpu.VMEM)
    field = (NB, VEC, BS)
    dma = pltpu.SemaphoreType.DMA
    corr, res = pl.pallas_call(
        kernel,
        out_shape=(pltpu.VMEM(field, F32), pltpu.VMEM(field, F32)),
        in_specs=[hbm] * 8,
        out_specs=(vmem, vmem),
        scratch_shapes=[
            pltpu.SMEM((NB, NS), jnp.int32),
            pltpu.SMEM((NB, NS), jnp.int32),
            pltpu.SMEM((4,), jnp.int32),
            pltpu.VMEM(field, F32),
            pltpu.VMEM((NB, BS), F32),
            pltpu.VMEM((NB, NS, BS, BS), F32),
            pltpu.VMEM((NB, BS), jnp.int32),
            pltpu.VMEM((ROWS, NG * NY * BS), F32),
            pltpu.VMEM((3,) + field, F32),
            pltpu.VMEM((3,) + field, F32),
            pltpu.VMEM((3,) + field, F32),
            pltpu.VMEM((3,) + field, F32),
            pltpu.VMEM((2 * NB, 2 * VEC, BS), BF16),
            pltpu.VMEM((NB, NS * BS, 2 * BS), BF16),
            pltpu.VMEM((3, 8, 8, BS), F32),
            pltpu.VMEM((NG, NY, ROWS, BS), F32),
            pltpu.VMEM((NG, NY, ROWS, BS), F32),
            pltpu.VMEM((NY, BS, 2 * BS), BF16),
            pltpu.VMEM((BS, NB * BS), BF16),
            pltpu.VMEM((BS, NB * BS), BF16),
            pltpu.VMEM((NX, 8, BS), F32),
            pltpu.VMEM((NZL, 2 * NX, 8, BS), F32),
            pltpu.VMEM((NY, VEC, BS), F32),
            pltpu.VMEM((2, 12, BS), F32),
            pltpu.VMEM((NZH, NG, 12, BS), F32),
            dma((11,)),
            dma((3, 2)), dma((3, 2)),
            dma((3, 8)), dma((3, 8)),
            dma((8,)), dma((8,)),
            dma((32,)), dma((32,)),
            dma((8,)), dma((8,)),
            dma((16,)), dma((16,)),
        ],
        compiler_params=pltpu.CompilerParams(collective_id=0, has_side_effects=True, vmem_limit_bytes=58 * 1024 * 1024),
    )(neighbors, slot_mask, send_list, loads, diagonal, stiffness, aggregate, coarse_inverse)
    corr = pltpu.with_memory_space_constraint(corr, pltpu.VMEM)
    res = pltpu.with_memory_space_constraint(res, pltpu.VMEM)
    return pl.pallas_call(
        store,
        out_shape=(jax.ShapeDtypeStruct(field, F32), jax.ShapeDtypeStruct(field, F32)),
        in_specs=[vmem, vmem],
        out_specs=(hbm, hbm),
        scratch_shapes=[dma((2,))],
    )(corr, res)


def solution(mesh):
    both = ("wide", "narrow")
    return jax.shard_map(
        shards,
        mesh=mesh,
        in_specs=(
            P(both, None, None),
            P(both, None),
            P(both, None, None, None),
            P(both, None),
            P(both, None),
            P(both),
            P(both, None),
            P(both, None),
        ),
        out_specs=(P(both, None, None), P(both, None, None)),
        check_vma=False,
    )
```
